256 devices in a mesh: seq: 32 (over x_hi, z, core), batch: 8 (over x_lo, y).
Axes of the slice: x: 4 (x_hi: 2, x_lo: 2; x = x_hi * 2 + x_lo), y: 4, z: 8, core: 2. Of those that a mesh axis runs over, the one named last changes fastest.
Arguments:
- bases: int32 [65536, 128], P(('batch', 'seq')), parts along dimension 0, may hold values from 0 to 3
- embed_table: bfloat16 [512, 768], replicated, may hold values from -0.5 to 0.5
- norm_gains: float32 [3, 768], replicated, may hold values from 0.1 to 1.9
- depth_taps: float32 [3, 5, 768], replicated, may hold values from -2.5 to 2.5
- point_weight: bfloat16 [3, 768, 768], replicated, may hold values from -0.21875 to 0.21875
- query_weight: bfloat16 [768, 128], replicated, may hold values from -0.5390625 to 0.5390625
- key_weight: bfloat16 [768, 128], replicated, may hold values from -0.5390625 to 0.5390625
- pair_kernel: bfloat16 [3, 3, 128, 128], replicated, may hold values from -0.1875 to 0.1875
Outputs:
- trunk: bfloat16 [65536, 768], P(('batch', 'seq')), parts along dimension 0
- pair_map: bfloat16 [4096, 512, 128], P(('batch', 'seq')), parts along dimension 0
The draws below stay inside these ranges and needn't reach their ends.
There are 8 independent parts, one for each index of `batch`. The reference program is written for one: setup_inputs(seed, part) draws one part's arguments, and reference() takes and returns one part's arrays. A program takes and returns all parts, laid end to end along the dimension named above; an argument that names none is the same for every part. Nothing has to cross between parts.
All inputs are finite; a program needn't handle non-finite values.
Results may differ from the reference program's by a relative error of at most 0.018.
Values may be sent and summed in bfloat16 or wider, within the bound.
No kernel may reach another device: no remote copies, remote signals or barrier semaphores. Data moves between devices by JAX's collectives and lax.ppermute only.
A program may use at most 64 MiB of HBM per device.

```python
import jax
import jax.numpy as jnp
from jax import lax

C = 768
PC = 128
BASES = 128
KW = 5
FIRST_DILATION = 2
SECOND_DILATION = 8
THIRD_DILATION = 32
POOL = 16
BINS = 8192


def with_ends(array, own_key, low, high):
    shape = array.shape
    place = [jax.random.randint(jax.random.fold_in(own_key, axis), (), 0, shape[axis]) for axis in range(len(shape))]
    array = array.at[tuple(place)].set(low)
    longest = shape.index(max(shape))
    place[longest] = (place[longest] + 1) % shape[longest]
    return array.at[tuple(place)].set(high)


def bell_draw(key, dims, spread, most, kind=jnp.bfloat16):
    entries = spread * jax.random.normal(key, dims, jnp.float32)
    return jnp.clip(entries, min=-most, max=most).astype(kind)


def setup_inputs(seed: int = 0, part: int = 0) -> dict:
    key_of = jax.random.split(jax.random.key(seed), 9)
    part_splits = jax.random.split(jax.random.fold_in(key_of[8], part), 9)
    bases = with_ends(jax.random.randint(part_splits[0], (BINS, BASES), 0, 4), jax.random.fold_in(part_splits[0], 1), 0, 3).astype(jnp.int32)
    embed_table = bell_draw(key_of[1], (4 * BASES, C), BASES ** -0.5, 0.5)
    norm_gains = jnp.clip(1.0 + 0.18 * jax.random.normal(key_of[2], (3, C), jnp.float32), 0.1, 1.9)
    depth_taps = bell_draw(key_of[3], (3, KW, C), KW ** -0.5, 2.5, jnp.float32)
    point_weight = bell_draw(key_of[4], (3, C, C), C ** -0.5, 0.21875)
    query_weight = bell_draw(key_of[5], (C, PC), (2.5 / C ** 0.5), 0.5390625)
    key_weight = bell_draw(key_of[6], (C, PC), (2.5 / C ** 0.5), 0.5390625)
    pair_kernel = bell_draw(key_of[7], (3, 3, PC, PC), (9 * PC) ** -0.5, 0.1875)
    return dict(bases=bases, embed_table=embed_table, norm_gains=norm_gains, depth_taps=depth_taps, point_weight=point_weight, query_weight=query_weight, key_weight=key_weight, pair_kernel=pair_kernel)


def embed_bases(bases, embed_table):
    one_hot_bases = (bases[:, :, None] == jnp.arange(4, dtype=jnp.int32)).astype(jnp.bfloat16)
    one_hot_bases = one_hot_bases.reshape(bases.shape[0], -1)
    return jnp.dot(one_hot_bases, embed_table, preferred_element_type=jnp.float32).astype(jnp.bfloat16)

def normalize(value_rows, gain):
    floats = value_rows.astype(jnp.float32)
    scale = lax.rsqrt(lax.optimization_barrier(jnp.mean(floats * floats, axis=-1, keepdims=True)) + 1e-06)
    return (floats * scale * gain).astype(jnp.bfloat16)

def mix_rows(inner, normed, taps, point, dilation_reach, rows):
    summed = jnp.zeros((rows, normed.shape[1]), jnp.float32)
    for offset in range(KW):
        summed = summed + normed[offset * dilation_reach:offset * dilation_reach + rows].astype(jnp.float32) * taps[offset]
    activated = jax.nn.gelu(summed).astype(jnp.bfloat16)
    return (inner.astype(jnp.float32) + jnp.dot(activated, point, preferred_element_type=jnp.float32)).astype(jnp.bfloat16)

def pair_conv(extended, pair_kernel, rows, width):
    padded = jnp.pad(extended, ((0, 0), (1, 1), (0, 0)))
    channels = extended.shape[2]
    summed = jnp.zeros((rows * width, channels), jnp.float32)
    for row_tap in range(3):
        for col_tap in range(3):
            window = padded[row_tap:row_tap + rows, col_tap:col_tap + width].reshape(rows * width, channels)
            summed = summed + jnp.dot(window, pair_kernel[row_tap, col_tap], preferred_element_type=jnp.float32)
    center = extended[1:rows + 1].astype(jnp.float32).reshape(rows * width, channels)
    return (center + jax.nn.gelu(summed)).astype(jnp.bfloat16).reshape(rows, width, channels)

def reference(bases, embed_table, norm_gains, depth_taps, point_weight, query_weight, key_weight, pair_kernel):
    current = embed_bases(bases, embed_table)
    total = current.shape[0]
    for trunk_layer, dilation_reach in enumerate((FIRST_DILATION, SECOND_DILATION, THIRD_DILATION)):
        normed = normalize(current, norm_gains[trunk_layer])
        padded = jnp.pad(normed, ((2 * dilation_reach, 2 * dilation_reach), (0, 0)))
        current = mix_rows(current, padded, depth_taps[trunk_layer], point_weight[trunk_layer], dilation_reach, total)
    trunk = current
    pooled = lax.optimization_barrier(jnp.mean(trunk.astype(jnp.float32).reshape(-1, POOL, trunk.shape[1]), axis=1)).astype(jnp.bfloat16)
    queries = jnp.dot(pooled, query_weight, preferred_element_type=jnp.float32).astype(jnp.bfloat16)
    keys = jnp.dot(pooled, key_weight, preferred_element_type=jnp.float32).astype(jnp.bfloat16)
    pair = (queries.astype(jnp.float32)[:, None, :] * keys.astype(jnp.float32)[None, :, :]).astype(jnp.bfloat16)
    extended = jnp.pad(pair, ((1, 1), (0, 0), (0, 0)))
    pair_map = pair_conv(extended, pair_kernel, pair.shape[0], pair.shape[1])
    return (trunk, pair_map)
```

```python
import math

import jax
import jax.numpy as jnp
from jax import lax
from jax.experimental import pallas as pl
from jax.experimental.pallas import tpu as pltpu
from jax.sharding import Mesh
from jax.sharding import PartitionSpec as P

F32 = jnp.float32
BF16 = jnp.bfloat16
C = 768
PC = 128
BASES = 128
BINS = 8192
SLAB = 256
POOL = 16
HALO = 112
ROWS = SLAB + 2 * HALO
DILATIONS = (2, 8, 32)
STARTS = (16, 32, 96)
ENDS = (464, 448, 384)
STEP = 16

GELU_A = math.sqrt(2.0 / math.pi)
GELU_B = 0.044715 * GELU_A


def gelu_of_half(half):
    squared = half * half
    inner = half * (2.0 * GELU_A + (8.0 * GELU_B) * squared)
    return half + half * jnp.tanh(inner)


def trunk_kernel(
    own, low, high, table_hbm, gains, taps, point_hbm, query_w, key_w,
    trunk_out, keys_out, query_out,
    x_ref, n_ref, a_ref, table, point, sems,
):
    copies = [pltpu.make_async_copy(table_hbm, table, sems.at[0])]
    for layer in range(3):
        copies.append(
            pltpu.make_async_copy(point_hbm.at[layer], point.at[layer], sems.at[1 + layer])
        )
    for copy in copies:
        copy.start()
    place = lax.axis_index(("x_hi", "z", "core"))
    first_bin = place * SLAB - HALO

    spread = (
        lax.broadcasted_iota(jnp.int32, (BASES, 4 * BASES), 1) // 4
        == lax.broadcasted_iota(jnp.int32, (BASES, 4 * BASES), 0)
    ).astype(F32).astype(BF16)
    copies[0].wait()

    def embed(codes, at, count):
        repeated = jnp.dot(codes.astype(F32).astype(BF16), spread, preferred_element_type=F32)
        base = (lax.broadcasted_iota(jnp.int32, (count, 4 * BASES), 1) % 4).astype(F32)
        one_hot = jnp.where(repeated == base, 1.0, 0.0).astype(BF16)
        x_ref[at : at + count, :] = jnp.dot(one_hot, table[...], preferred_element_type=F32)

    embed(low[...], 0, HALO)
    embed(own[0:128, :], HALO, 128)
    embed(own[128:256, :], HALO + 128, 128)
    embed(high[...], HALO + SLAB, HALO)

    for layer in range(3):
        reach = DILATIONS[layer]
        in_start = STARTS[layer] - max(8, 2 * reach)
        in_end = ENDS[layer] + max(8, 2 * reach)
        gain = gains[layer : layer + 1, :]

        def norm_step(j, _, in_start=in_start, gain=gain):
            at = pl.multiple_of(in_start + j * STEP, 8)
            rows = x_ref[pl.ds(at, STEP), :]
            mean = jnp.sum(rows * rows, axis=-1, keepdims=True) * (1.0 / C)
            bins = first_bin + at + lax.broadcasted_iota(jnp.int32, (STEP, 1), 0)
            inside = (bins >= 0) & (bins < BINS)
            scale = jnp.where(inside, lax.rsqrt(mean + 1e-06), 0.0)
            n_ref[pl.ds(at, STEP), :] = rows * scale * gain
            return 0

        lax.fori_loop(0, (in_end - in_start) // STEP, norm_step, 0, unroll=2)

        tap_rows = [taps[layer, t : t + 1, :] * 0.5 for t in range(5)]
        start = STARTS[layer]

        def conv_step(j, _, start=start, reach=reach, tap_rows=tap_rows):
            at = pl.multiple_of(start + j * STEP, 8)
            if reach % 8:
                wide = n_ref[pl.ds(pl.multiple_of(at - 8, 8), STEP + 16), :]
                pieces = [wide[8 + (t - 2) * reach : 8 + (t - 2) * reach + STEP] for t in range(5)]
            else:
                pieces = [
                    n_ref[pl.ds(pl.multiple_of(at + (t - 2) * reach, 8), STEP), :] for t in range(5)
                ]
            half = pieces[0] * tap_rows[0]
            for t in range(1, 5):
                half = half + pieces[t] * tap_rows[t]
            a_ref[pl.ds(pl.multiple_of(at, 16), STEP), :] = gelu_of_half(half).astype(BF16)
            return 0

        lax.fori_loop(0, (ENDS[layer] - start) // STEP, conv_step, 0, unroll=2)
        copies[1 + layer].wait()
        for strip in range(3):
            cols = slice(strip * 256, strip * 256 + 256)
            update = jnp.dot(
                a_ref[start : ENDS[layer], :], point[layer, :, cols], preferred_element_type=F32
            )
            total = x_ref[start : ENDS[layer], cols] + update
            if layer < 2:
                x_ref[start : ENDS[layer], cols] = total
            else:
                n_ref[start : ENDS[layer], cols] = total

    trunk = n_ref[STARTS[2] : ENDS[2], :].astype(BF16)
    trunk_out[...] = trunk[POOL : POOL + SLAB, :]
    count = ENDS[2] - STARTS[2]
    pooling = jnp.where(
        lax.broadcasted_iota(jnp.int32, (32, count), 1) // POOL
        == lax.broadcasted_iota(jnp.int32, (32, count), 0),
        1.0 / POOL,
        0.0,
    ).astype(BF16)
    pooled = jnp.dot(pooling, trunk, preferred_element_type=F32).astype(BF16)
    queries = jnp.dot(pooled, query_w[...], preferred_element_type=F32).astype(BF16).astype(F32)
    keys = jnp.dot(pooled, key_w[...], preferred_element_type=F32)
    row = place * (SLAB // POOL) - 1 + lax.broadcasted_iota(jnp.int32, (32, PC), 0)
    query_out[...] = jnp.where((row >= 0) & (row < BINS // POOL), queries, 0.0)
    mine = pltpu.roll(keys, 31, 0)[0:16].astype(BF16)
    for peer in range(16):
        keys_out[peer] = mine


def pair_kernel_body(
    queries, own, other, kernel, out_hbm, wide_q, kernel_f, key_f, key_cat, out_ref, weights, sems
):
    core = lax.axis_index("core")
    flipped = jnp.transpose(queries[...], (1, 0))
    for i in range(18):
        wide_q[i] = jnp.broadcast_to(flipped[:, i : i + 1] * 0.5, (PC, PC))
    for t in range(9):
        kernel_f[t] = kernel[t // 3, t % 3].astype(F32)
    for g in range(16):
        mine = own[g]
        theirs = other[g]
        key_cat[g * 32 : g * 32 + 16, PC : 2 * PC] = jnp.where(core == 0, mine, theirs)
        key_cat[g * 32 + 16 : g * 32 + 32, PC : 2 * PC] = jnp.where(core == 0, theirs, mine)
    keys = key_cat[:, PC : 2 * PC].astype(F32)
    key_f[...] = keys
    at = lax.broadcasted_iota(jnp.int32, keys.shape, 0)
    before = jnp.where(at == 0, 0.0, pltpu.roll(keys, 1, 0))
    after = jnp.where(at == 511, 0.0, pltpu.roll(keys, 511, 0))
    key_cat[:, 0:PC] = before.astype(BF16)
    key_cat[:, 2 * PC : 3 * PC] = after.astype(BF16)

    def copy_of(i):
        return pltpu.make_async_copy(
            out_ref.at[pl.ds(2 * i, 2)], out_hbm.at[pl.ds(2 * i, 2)], sems.at[i]
        )

    def two_rows(i, _):
        for r in range(2):
            row = 2 * i + r
            for b in range(3):
                mixed = wide_q[row] * kernel_f[b]
                mixed = mixed + wide_q[row + 1] * kernel_f[3 + b]
                mixed = mixed + wide_q[row + 2] * kernel_f[6 + b]
                weights[b * PC : (b + 1) * PC, r * PC : (r + 1) * PC] = mixed.astype(BF16)
        for m in range(4):
            rows = slice(m * 128, m * 128 + 128)
            half = jnp.dot(key_cat[rows, :], weights[...], preferred_element_type=F32)
            for r in range(2):
                query = queries[pl.ds(2 * i + r + 1, 1), :]
                pair = key_f[rows, :] * query
                value = pair + gelu_of_half(half[:, r * PC : (r + 1) * PC])
                out_ref[2 * i + r, rows, :] = value.astype(BF16)
        copy_of(i).start()
        return 0

    lax.fori_loop(0, 8, two_rows, 0)

    def finish(i, _):
        copy_of(i).wait()
        return 0

    lax.fori_loop(0, 8, finish, 0)


def vmem(count):
    return [pl.BlockSpec(memory_space=pltpu.VMEM)] * count


def on_device(
    bases, embed_table, norm_gains, depth_taps, point_weight, query_weight, key_weight, pair_kernel
):
    core = lax.axis_index("core")
    seq = ("x_hi", "z", "core")
    head_first = jnp.where(core == 0, SLAB - HALO, 0)
    inner_send = lax.dynamic_slice(bases, (head_first, 0), (HALO, BASES))
    outer_send = lax.dynamic_slice(bases, (SLAB - HALO - head_first, 0), (HALO, BASES))
    outer_pairs = []
    for i in range(1, 31, 2):
        outer_pairs += [(i, i + 1), (i + 1, i)]
    outer = lax.ppermute(outer_send, seq, outer_pairs)
    inner = lax.ppermute(inner_send, "core", [(0, 1), (1, 0)])
    low = jnp.where(core == 0, outer, inner)
    high = jnp.where(core == 0, inner, outer)

    any_space = [pl.BlockSpec(memory_space=pl.ANY)]
    trunk, keys, queries = pl.pallas_call(
        trunk_kernel,
        out_shape=(
            jax.ShapeDtypeStruct((SLAB, C), BF16),
            jax.ShapeDtypeStruct((16, 16, PC), BF16),
            jax.ShapeDtypeStruct((32, PC), F32),
        ),
        in_specs=vmem(3) + any_space + vmem(2) + any_space + vmem(2),
        out_specs=tuple(vmem(3)),
        scratch_shapes=[
            pltpu.VMEM((ROWS, C), F32),
            pltpu.VMEM((ROWS, C), F32),
            pltpu.VMEM((ROWS, C), BF16),
            pltpu.VMEM((4 * BASES, C), BF16),
            pltpu.VMEM((3, C, C), BF16),
            pltpu.SemaphoreType.DMA((4,)),
        ],
        compiler_params=pltpu.CompilerParams(vmem_limit_bytes=40 * 1024 * 1024),
        name="trunk",
    )(bases, low, high, embed_table, norm_gains, depth_taps, point_weight, query_weight, key_weight)

    own_keys = lax.all_to_all(keys, ("x_hi", "z"), 0, 0, tiled=False)
    other_keys = lax.ppermute(own_keys, "core", [(0, 1), (1, 0)])

    pair_map = pl.pallas_call(
        pair_kernel_body,
        out_shape=jax.ShapeDtypeStruct((16, 512, PC), BF16),
        in_specs=vmem(4),
        out_specs=pl.BlockSpec(memory_space=pl.ANY),
        scratch_shapes=[
            pltpu.VMEM((18, PC, PC), F32),
            pltpu.VMEM((9, PC, PC), F32),
            pltpu.VMEM((512, PC), F32),
            pltpu.VMEM((512, 3 * PC), BF16),
            pltpu.VMEM((16, 512, PC), BF16),
            pltpu.VMEM((3 * PC, 2 * PC), BF16),
            pltpu.SemaphoreType.DMA((8,)),
        ],
        compiler_params=pltpu.CompilerParams(vmem_limit_bytes=24 * 1024 * 1024),
        name="pair",
    )(queries, own_keys, other_keys, pair_kernel)
    return (trunk, pair_map)


def solution(mesh):
    devices = mesh.devices.reshape(2, 8, 2, -1)
    fine = Mesh(devices, ("x_hi", "z", "core", "batch"))
    rows = ("batch", "x_hi", "z", "core")
    return jax.shard_map(
        on_device,
        mesh=fine,
        in_specs=(P(rows, None), P(), P(), P(), P(), P(), P(), P()),
        out_specs=(P(rows, None), P(rows, None, None)),
        check_vma=False,
    )
```

```python
import math

import jax
import jax.numpy as jnp
from jax import lax
from jax.experimental import pallas as pl
from jax.experimental.pallas import tpu as pltpu
from jax.sharding import Mesh
from jax.sharding import PartitionSpec as P

F32 = jnp.float32
BF16 = jnp.bfloat16
C = 768
PC = 128
BASES = 128
BINS = 8192
SLAB = 256
POOL = 16
HALO = 112
ROWS = SLAB + 2 * HALO
DILATIONS = (2, 8, 32)
STEP = 16

GELU_A = math.sqrt(2.0 / math.pi)
GELU_B = 0.044715 * GELU_A


def gelu_of_half(half):
    squared = half * half
    inner = half * (2.0 * GELU_A + (8.0 * GELU_B) * squared)
    return half + half * jnp.tanh(inner)


def spread_matrix():
    return (
        lax.broadcasted_iota(jnp.int32, (BASES, 4 * BASES), 1) // 4
        == lax.broadcasted_iota(jnp.int32, (BASES, 4 * BASES), 0)
    ).astype(F32).astype(BF16)


def embed(codes, spread, table):
    repeated = jnp.dot(codes.astype(F32).astype(BF16), spread, preferred_element_type=F32)
    base = (lax.broadcasted_iota(jnp.int32, repeated.shape, 1) % 4).astype(F32)
    one_hot = jnp.where(repeated == base, 1.0, 0.0).astype(BF16)
    return jnp.dot(one_hot, table[...], preferred_element_type=F32)


def norm_rows(x_ref, n_ref, layer, count, row_of, scale_of, unroll):
    def step(j, _):
        at = pl.multiple_of(row_of(j), STEP)
        rows = x_ref[pl.ds(at, STEP), :]
        mean = jnp.sum(rows * rows, axis=-1, keepdims=True) * (1.0 / C)
        rows = rows * (lax.rsqrt(mean + 1e-06) * scale_of(at))
        for c in range(C // 128):
            n_ref[layer, c, pl.ds(at, STEP), :] = rows[:, c * 128 : (c + 1) * 128]
        return 0

    lax.fori_loop(0, count, step, 0, unroll=unroll)


def conv_rows(n_ref, a_ref, layer, gains, taps, count, row_of, unroll):
    reach = DILATIONS[layer]
    gain = gains[layer : layer + 1, :] * 0.5
    tap_rows = [taps[t, layer : layer + 1, :] * gain for t in range(5)]

    def step(j, _):
        at = row_of(j)
        to = pl.multiple_of(j * STEP, STEP)
        for c in range(C // 128):
            cols = slice(c * 128, (c + 1) * 128)
            half = None
            for t in range(5):
                piece = n_ref[layer, c, pl.ds(at + (t - 2) * reach, STEP), :]
                term = piece * tap_rows[t][:, cols]
                half = term if half is None else half + term
            a_ref[pl.ds(to, STEP), cols] = gelu_of_half(half).astype(BF16)
        return 0

    lax.fori_loop(0, count, step, 0, unroll=unroll)


def mix(a_ref, x_ref, weights, spans):
    total = sum(stop - start for start, stop in spans)
    for strip in range(3):
        cols = slice(strip * 256, strip * 256 + 256)
        update = jnp.dot(a_ref[0:total, :], weights[:, cols], preferred_element_type=F32)
        done = 0
        for start, stop in spans:
            x_ref[start:stop, cols] = x_ref[start:stop, cols] + update[done : done + stop - start]
            done += stop - start


def inner_kernel(own, table_hbm, gains, taps, point_hbm, x_ref, n_ref, table, point, a_ref, sems):
    copies = [pltpu.make_async_copy(table_hbm, table, sems.at[0])]
    for layer in range(3):
        copies.append(
            pltpu.make_async_copy(point_hbm.at[layer], point.at[layer], sems.at[1 + layer])
        )
    for copy in copies:
        copy.start()
    spread = spread_matrix()
    copies[0].wait()
    for half in range(2):
        at = HALO + half * 128
        x_ref[at : at + 128, :] = embed(own[half * 128 : half * 128 + 128, :], spread, table)

    def one(at):
        return 1.0

    norm_rows(x_ref, n_ref, 0, 16, lambda j: HALO + j * STEP, one, 4)
    conv_rows(n_ref, a_ref, 0, gains, taps, 14, lambda j: 128 + j * STEP, 2)
    copies[1].wait()
    mix(a_ref, x_ref, point.at[0], ((128, 352),))
    norm_rows(x_ref, n_ref, 1, 14, lambda j: 128 + j * STEP, one, 7)
    conv_rows(n_ref, a_ref, 1, gains, taps, 12, lambda j: 144 + j * STEP, 2)
    copies[2].wait()
    mix(a_ref, x_ref, point.at[1], ((144, 336),))
    norm_rows(x_ref, n_ref, 2, 12, lambda j: 144 + j * STEP, one, 4)
    copies[3].wait()


def outer_kernel(
    inner, outer, gains, taps, table, point, query_w, key_w, x_in, n_in,
    trunk_out, keys_out, query_out, x_ref, n_ref, a_ref,
):
    del x_in, n_in
    place = lax.axis_index(("x_hi", "z", "core"))
    core = lax.axis_index("core")
    low_bases = jnp.where(core == 0, outer[SLAB - HALO :, :], inner[SLAB - HALO :, :])
    high_bases = jnp.where(core == 0, inner[:HALO, :], outer[:HALO, :])
    spread = spread_matrix()
    both = embed(jnp.concatenate([low_bases, high_bases], axis=0), spread, table)
    x_ref[0:HALO, :] = both[0:HALO]
    x_ref[HALO + SLAB :, :] = both[HALO:]

    def inside(at):
        gone = ((at < HALO) & (place == 0)) | ((at >= HALO + SLAB) & (place == 31))
        return jnp.where(gone, 0.0, 1.0)

    def two_spans(low, high):
        return lambda j: jnp.where(j < 7, low + j * STEP, high + (j - 7) * STEP)

    norm_rows(x_ref, n_ref, 0, 14, two_spans(0, 368), inside, 7)
    conv_rows(n_ref, a_ref, 0, gains, taps, 14, two_spans(16, 352), 2)
    mix(a_ref, x_ref, point.at[0], ((16, 128), (352, 464)))
    norm_rows(x_ref, n_ref, 1, 14, two_spans(16, 352), inside, 7)
    conv_rows(n_ref, a_ref, 1, gains, taps, 14, two_spans(32, 336), 2)
    mix(a_ref, x_ref, point.at[1], ((32, 144), (336, 448)))
    norm_rows(x_ref, n_ref, 2, 14, two_spans(32, 336), inside, 7)
    conv_rows(n_ref, a_ref, 2, gains, taps, 18, lambda j: 96 + j * STEP, 2)
    mix(a_ref, x_ref, point.at[2], ((96, 384),))

    trunk = x_ref[96:384, :].astype(BF16)
    trunk_out[...] = trunk[POOL : POOL + SLAB, :]
    pooling = jnp.where(
        lax.broadcasted_iota(jnp.int32, (32, 288), 1) // POOL
        == lax.broadcasted_iota(jnp.int32, (32, 288), 0),
        1.0 / POOL,
        0.0,
    ).astype(BF16)
    pooled = jnp.dot(pooling, trunk, preferred_element_type=F32).astype(BF16)
    queries = jnp.dot(pooled, query_w[...], preferred_element_type=F32).astype(BF16).astype(F32)
    keys = jnp.dot(pooled, key_w[...], preferred_element_type=F32)
    row = place * (SLAB // POOL) - 1 + lax.broadcasted_iota(jnp.int32, (32, PC), 0)
    query_out[...] = jnp.where((row >= 0) & (row < BINS // POOL), queries, 0.0)
    mine = pltpu.roll(keys, 31, 0)[0:16].astype(BF16)
    for peer in range(16):
        keys_out[peer] = mine


def pair_kernel_body(
    queries, own, other, kernel, out_hbm, wide_q, kernel_f, key_f, key_cat, out_ref, weights, sems
):
    core = lax.axis_index("core")
    flipped = jnp.transpose(queries[...], (1, 0))
    for i in range(18):
        wide_q[i] = jnp.broadcast_to(flipped[:, i : i + 1] * 0.5, (PC, PC))
    for t in range(9):
        kernel_f[t] = kernel[t // 3, t % 3].astype(F32)
    for g in range(16):
        mine = own[g]
        theirs = other[g]
        key_cat[g * 32 : g * 32 + 16, PC : 2 * PC] = jnp.where(core == 0, mine, theirs)
        key_cat[g * 32 + 16 : g * 32 + 32, PC : 2 * PC] = jnp.where(core == 0, theirs, mine)
    keys = key_cat[:, PC : 2 * PC].astype(F32)
    key_f[...] = keys
    at = lax.broadcasted_iota(jnp.int32, keys.shape, 0)
    before = jnp.where(at == 0, 0.0, pltpu.roll(keys, 1, 0))
    after = jnp.where(at == 511, 0.0, pltpu.roll(keys, 511, 0))
    key_cat[:, 0:PC] = before.astype(BF16)
    key_cat[:, 2 * PC : 3 * PC] = after.astype(BF16)

    def copy_of(i):
        return pltpu.make_async_copy(
            out_ref.at[pl.ds(2 * i, 2)], out_hbm.at[pl.ds(2 * i, 2)], sems.at[i]
        )

    def two_rows(i, _):
        for r in range(2):
            row = 2 * i + r
            for b in range(3):
                mixed = wide_q[row] * kernel_f[b]
                mixed = mixed + wide_q[row + 1] * kernel_f[3 + b]
                mixed = mixed + wide_q[row + 2] * kernel_f[6 + b]
                weights[b * PC : (b + 1) * PC, r * PC : (r + 1) * PC] = mixed.astype(BF16)
        for m in range(4):
            rows = slice(m * 128, m * 128 + 128)
            half = jnp.dot(key_cat[rows, :], weights[...], preferred_element_type=F32)
            for r in range(2):
                query = queries[pl.ds(2 * i + r + 1, 1), :]
                pair = key_f[rows, :] * query
                value = pair + gelu_of_half(half[:, r * PC : (r + 1) * PC])
                out_ref[2 * i + r, rows, :] = value.astype(BF16)
        copy_of(i).start()
        return 0

    lax.fori_loop(0, 8, two_rows, 0)

    def finish(i, _):
        copy_of(i).wait()
        return 0

    lax.fori_loop(0, 8, finish, 0)


def in_hbm(array):
    return pltpu.with_memory_space_constraint(array, pltpu.HBM)


def vmem(count):
    return [pl.BlockSpec(memory_space=pltpu.VMEM)] * count


def on_device(
    bases, embed_table, norm_gains, depth_taps, point_weight, query_weight, key_weight, pair_kernel
):
    seq = ("x_hi", "z", "core")
    outer_pairs = []
    for i in range(1, 31, 2):
        outer_pairs += [(i, i + 1), (i + 1, i)]
    inner = lax.ppermute(bases, "core", [(0, 1), (1, 0)])
    outer = lax.ppermute(bases, seq, outer_pairs)

    taps = jnp.transpose(depth_taps, (1, 0, 2))
    hbm_space = [pl.BlockSpec(memory_space=pltpu.HBM)]
    state = (
        jax.ShapeDtypeStruct((ROWS, C), F32),
        jax.ShapeDtypeStruct((3, C // 128, ROWS, 128), F32),
    )
    x, n, table, point = pl.pallas_call(
        inner_kernel,
        out_shape=state
        + (
            jax.ShapeDtypeStruct((4 * BASES, C), BF16),
            jax.ShapeDtypeStruct((3, C, C), BF16),
        ),
        in_specs=vmem(1) + hbm_space + vmem(2) + hbm_space,
        out_specs=tuple(vmem(4)),
        scratch_shapes=[pltpu.VMEM((SLAB, C), BF16), pltpu.SemaphoreType.DMA((4,))],
        compiler_params=pltpu.CompilerParams(vmem_limit_bytes=16 * 1024 * 1024),
        cost_estimate=pl.CostEstimate(
            flops=800_000_000, bytes_accessed=5_000_000, transcendentals=400_000
        ),
        name="inner",
    )(in_hbm(bases), in_hbm(embed_table), in_hbm(norm_gains), in_hbm(taps), in_hbm(point_weight))
    trunk, keys, queries, _, _ = pl.pallas_call(
        outer_kernel,
        out_shape=(
            jax.ShapeDtypeStruct((SLAB, C), BF16),
            jax.ShapeDtypeStruct((16, 16, PC), BF16),
            jax.ShapeDtypeStruct((32, PC), F32),
        )
        + state,
        in_specs=vmem(10),
        out_specs=tuple(vmem(5)),
        scratch_shapes=[pltpu.VMEM((288, C), BF16)],
        input_output_aliases={8: 3, 9: 4},
        compiler_params=pltpu.CompilerParams(vmem_limit_bytes=16 * 1024 * 1024),
        cost_estimate=pl.CostEstimate(
            flops=1_000_000_000, bytes_accessed=1_000_000, transcendentals=600_000
        ),
        name="outer",
    )(inner, outer, norm_gains, taps, table, point, query_weight, key_weight, x, n)

    own_keys = lax.all_to_all(keys, ("x_hi", "z"), 0, 0, tiled=False)
    other_keys = lax.ppermute(own_keys, "core", [(0, 1), (1, 0)])

    pair_map = pl.pallas_call(
        pair_kernel_body,
        out_shape=jax.ShapeDtypeStruct((16, 512, PC), BF16),
        in_specs=vmem(4),
        out_specs=pl.BlockSpec(memory_space=pl.ANY),
        scratch_shapes=[
            pltpu.VMEM((18, PC, PC), F32),
            pltpu.VMEM((9, PC, PC), F32),
            pltpu.VMEM((512, PC), F32),
            pltpu.VMEM((512, 3 * PC), BF16),
            pltpu.VMEM((16, 512, PC), BF16),
            pltpu.VMEM((3 * PC, 2 * PC), BF16),
            pltpu.SemaphoreType.DMA((8,)),
        ],
        compiler_params=pltpu.CompilerParams(vmem_limit_bytes=24 * 1024 * 1024),
        name="pair",
    )(queries, own_keys, other_keys, pair_kernel)
    return (trunk, pair_map)


def solution(mesh):
    devices = mesh.devices.reshape(2, 8, 2, -1)
    fine = Mesh(devices, ("x_hi", "z", "core", "batch"))
    rows = ("batch", "x_hi", "z", "core")
    return jax.shard_map(
        on_device,
        mesh=fine,
        in_specs=(P(rows, None), P(), P(), P(), P(), P(), P(), P()),
        out_specs=(P(rows, None), P(rows, None, None)),
        check_vma=False,
    )
```

```python
import math

import jax
import jax.numpy as jnp
from jax import lax
from jax.experimental import pallas as pl
from jax.experimental.pallas import tpu as pltpu
from jax.sharding import Mesh
from jax.sharding import PartitionSpec as P

F32 = jnp.float32
BF16 = jnp.bfloat16
C = 768
PC = 128
BASES = 128
BINS = 8192
SLAB = 256
POOL = 16
HALO = 112
ROWS = SLAB + 2 * HALO
DILATIONS = (2, 8, 32)
STEP = 16

GELU_A = math.sqrt(2.0 / math.pi)
GELU_B = 0.044715 * GELU_A


def gelu_of_half(half):
    half = half.astype(BF16)
    squared = half * half
    inner = half * (jnp.asarray(2.0 * GELU_A, BF16) + jnp.asarray(8.0 * GELU_B, BF16) * squared)
    return half + half * jnp.tanh(inner)


def spread_matrix():
    return (
        lax.broadcasted_iota(jnp.int32, (BASES, 4 * BASES), 1) // 4
        == lax.broadcasted_iota(jnp.int32, (BASES, 4 * BASES), 0)
    ).astype(F32).astype(BF16)


def one_hot_rows(codes, spread):
    repeated = jnp.dot(codes.astype(F32).astype(BF16), spread, preferred_element_type=F32)
    base = (lax.broadcasted_iota(jnp.int32, repeated.shape, 1) % 4).astype(F32)
    return jnp.where(repeated == base, 1.0, 0.0).astype(BF16)


def norm_rows(x_ref, n_ref, layer, count, row_of, scale_of, unroll):
    def step(j, _):
        at = pl.multiple_of(row_of(j), STEP)
        rows = x_ref[pl.ds(at, STEP), :]
        mean = jnp.sum(rows * rows, axis=-1, keepdims=True) * (1.0 / C)
        rows = rows * (lax.rsqrt(mean + 1e-06) * scale_of(at))
        for c in range(C // 128):
            n_ref[layer, c, pl.ds(at, STEP), :] = rows[:, c * 128 : (c + 1) * 128]
        return 0

    lax.fori_loop(0, count, step, 0, unroll=unroll)


def conv_rows(n_ref, a_ref, layer, gains, taps, count, row_of, unroll):
    reach = DILATIONS[layer]
    gain = gains[layer : layer + 1, :] * 0.5
    tap_rows = [taps[t, layer : layer + 1, :] * gain for t in range(5)]

    def step(j, _):
        at = row_of(j)
        to = pl.multiple_of(j * STEP, STEP)
        for c in range(C // 128):
            cols = slice(c * 128, (c + 1) * 128)
            half = None
            for t in range(5):
                piece = n_ref[layer, c, pl.ds(at + (t - 2) * reach, STEP), :]
                term = piece * tap_rows[t][:, cols]
                half = term if half is None else half + term
            a_ref[pl.ds(to, STEP), cols] = gelu_of_half(half)
        return 0

    lax.fori_loop(0, count, step, 0, unroll=unroll)


def mix(a_ref, x_ref, weights, spans):
    total = sum(stop - start for start, stop in spans)
    for strip in range(3):
        cols = slice(strip * 256, strip * 256 + 256)
        update = jnp.dot(a_ref[0:total, :], weights[:, cols], preferred_element_type=F32)
        done = 0
        for start, stop in spans:
            x_ref[start:stop, cols] = x_ref[start:stop, cols] + update[done : done + stop - start]
            done += stop - start


def inner_kernel(
    own_hbm, table_hbm, gains_hbm, taps_hbm, point_hbm,
    x_ref, n_ref, table, point,
    own, gains, taps, a_ref, sems,
):
    moves = [(own_hbm, own), (table_hbm, table), (gains_hbm, gains), (taps_hbm, taps)]
    moves += [(point_hbm.at[layer], point.at[layer]) for layer in range(3)]
    copies = [
        pltpu.make_async_copy(source, target, sems.at[k])
        for k, (source, target) in enumerate(moves)
    ]
    for copy in copies:
        copy.start()
    spread = spread_matrix()
    copies[0].wait()
    for half in range(2):
        rows = slice(half * 128, half * 128 + 128)
        a_ref[rows, 0 : 4 * BASES] = one_hot_rows(own[rows, :], spread)
    copies[1].wait()
    x_ref[HALO : HALO + SLAB, :] = jnp.dot(
        a_ref[:, 0 : 4 * BASES], table[...], preferred_element_type=F32
    )
    copies[2].wait()
    copies[3].wait()

    def one(at):
        return 1.0

    norm_rows(x_ref, n_ref, 0, 16, lambda j: HALO + j * STEP, one, 4)
    conv_rows(n_ref, a_ref, 0, gains, taps, 14, lambda j: 128 + j * STEP, 2)
    copies[4].wait()
    mix(a_ref, x_ref, point.at[0], ((128, 352),))
    norm_rows(x_ref, n_ref, 1, 14, lambda j: 128 + j * STEP, one, 7)
    conv_rows(n_ref, a_ref, 1, gains, taps, 12, lambda j: 144 + j * STEP, 2)
    copies[5].wait()
    mix(a_ref, x_ref, point.at[1], ((144, 336),))
    norm_rows(x_ref, n_ref, 2, 12, lambda j: 144 + j * STEP, one, 4)
    copies[6].wait()


def outer_kernel(
    inner, outer, gains, taps, table, point, query_w, key_w, x_in, n_in,
    trunk_out, keys_out, query_out, x_ref, n_ref, a_ref,
):
    del x_in, n_in
    place = lax.axis_index(("x_hi", "z", "core"))
    core = lax.axis_index("core")
    low_bases = jnp.where(core == 0, outer[SLAB - HALO :, :], inner[SLAB - HALO :, :])
    high_bases = jnp.where(core == 0, inner[:HALO, :], outer[:HALO, :])
    spread = spread_matrix()
    both = one_hot_rows(jnp.concatenate([low_bases, high_bases], axis=0), spread)
    both = jnp.dot(both, table[...], preferred_element_type=F32)
    x_ref[0:HALO, :] = both[0:HALO]
    x_ref[HALO + SLAB :, :] = both[HALO:]

    def inside(at):
        gone = ((at < HALO) & (place == 0)) | ((at >= HALO + SLAB) & (place == 31))
        return jnp.where(gone, 0.0, 1.0)

    def two_spans(low, high):
        return lambda j: jnp.where(j < 7, low + j * STEP, high + (j - 7) * STEP)

    norm_rows(x_ref, n_ref, 0, 14, two_spans(0, 368), inside, 7)
    conv_rows(n_ref, a_ref, 0, gains, taps, 14, two_spans(16, 352), 2)
    mix(a_ref, x_ref, point.at[0], ((16, 128), (352, 464)))
    norm_rows(x_ref, n_ref, 1, 14, two_spans(16, 352), inside, 7)
    conv_rows(n_ref, a_ref, 1, gains, taps, 14, two_spans(32, 336), 2)
    mix(a_ref, x_ref, point.at[1], ((32, 144), (336, 448)))
    norm_rows(x_ref, n_ref, 2, 14, two_spans(32, 336), inside, 7)
    conv_rows(n_ref, a_ref, 2, gains, taps, 18, lambda j: 96 + j * STEP, 2)
    mix(a_ref, x_ref, point.at[2], ((96, 384),))

    trunk = x_ref[96:384, :].astype(BF16)
    trunk_out[...] = trunk[POOL : POOL + SLAB, :]
    pooling = jnp.where(
        lax.broadcasted_iota(jnp.int32, (32, 288), 1) // POOL
        == lax.broadcasted_iota(jnp.int32, (32, 288), 0),
        1.0 / POOL,
        0.0,
    ).astype(BF16)
    pooled = jnp.dot(pooling, trunk, preferred_element_type=F32).astype(BF16)
    queries = jnp.dot(pooled, query_w[...], preferred_element_type=F32).astype(BF16).astype(F32)
    keys = jnp.dot(pooled, key_w[...], preferred_element_type=F32)
    row = place * (SLAB // POOL) - 1 + lax.broadcasted_iota(jnp.int32, (32, PC), 0)
    query_out[...] = jnp.where((row >= 0) & (row < BINS // POOL), queries, 0.0)
    mine = pltpu.roll(keys, 31, 0)[0:16].astype(BF16)
    for peer in range(16):
        keys_out[peer] = mine


def weights_kernel(queries, kernel, weights, wide_q):
    flipped = jnp.transpose(queries[...], (1, 0)) * 0.5
    for i in range(18):
        wide_q[i] = jnp.broadcast_to(flipped[:, i : i + 1], (PC, PC)).astype(BF16)

    def two_rows(i, _):
        for r in range(2):
            row = 2 * i + r
            for b in range(3):
                mixed = wide_q[row] * kernel[0, b]
                mixed = mixed + wide_q[row + 1] * kernel[1, b]
                mixed = mixed + wide_q[row + 2] * kernel[2, b]
                weights[i, b * PC : (b + 1) * PC, r * PC : (r + 1) * PC] = mixed
        return 0

    lax.fori_loop(0, 8, two_rows, 0)


def pair_kernel_body(queries, own, other, weights, out_hbm, key_cat, out_ref, sems):
    core = lax.axis_index("core")
    for g in range(16):
        mine = own[g]
        theirs = other[g]
        key_cat[g * 32 : g * 32 + 16, PC : 2 * PC] = jnp.where(core == 0, mine, theirs)
        key_cat[g * 32 + 16 : g * 32 + 32, PC : 2 * PC] = jnp.where(core == 0, theirs, mine)
    keys = key_cat[:, PC : 2 * PC].astype(F32)
    at = lax.broadcasted_iota(jnp.int32, keys.shape, 0)
    before = jnp.where(at == 0, 0.0, pltpu.roll(keys, 1, 0))
    after = jnp.where(at == 511, 0.0, pltpu.roll(keys, 511, 0))
    key_cat[:, 0:PC] = before.astype(BF16)
    key_cat[:, 2 * PC : 3 * PC] = after.astype(BF16)

    def copy_of(i):
        return pltpu.make_async_copy(
            out_ref.at[pl.ds(2 * i, 2)], out_hbm.at[pl.ds(2 * i, 2)], sems.at[i]
        )

    def two_rows(i, _):
        for m in range(2):
            rows = slice(m * 256, m * 256 + 256)
            half = jnp.dot(key_cat[rows, :], weights[i], preferred_element_type=F32)
            for r in range(2):
                query = queries[pl.ds(2 * i + r + 1, 1), :].astype(BF16)
                pair = key_cat[rows, PC : 2 * PC] * query
                out_ref[2 * i + r, rows, :] = pair + gelu_of_half(half[:, r * PC : (r + 1) * PC])
        copy_of(i).start()
        return 0

    lax.fori_loop(0, 8, two_rows, 0)

    def finish(i, _):
        copy_of(i).wait()
        return 0

    lax.fori_loop(0, 8, finish, 0)


def in_hbm(array):
    return pltpu.with_memory_space_constraint(array, pltpu.HBM)


def vmem(count):
    return [pl.BlockSpec(memory_space=pltpu.VMEM)] * count


def on_device(
    bases, embed_table, norm_gains, depth_taps, point_weight, query_weight, key_weight, pair_kernel
):
    seq = ("x_hi", "z", "core")
    outer_pairs = []
    for i in range(1, 31, 2):
        outer_pairs += [(i, i + 1), (i + 1, i)]
    inner = lax.ppermute(bases, "core", [(0, 1), (1, 0)])
    outer = lax.ppermute(bases, seq, outer_pairs)

    taps = jnp.transpose(depth_taps, (1, 0, 2))
    hbm_space = [pl.BlockSpec(memory_space=pltpu.HBM)]
    state = (
        jax.ShapeDtypeStruct((ROWS, C), F32),
        jax.ShapeDtypeStruct((3, C // 128, ROWS, 128), F32),
    )
    x, n, table, point = pl.pallas_call(
        inner_kernel,
        out_shape=state
        + (
            jax.ShapeDtypeStruct((4 * BASES, C), BF16),
            jax.ShapeDtypeStruct((3, C, C), BF16),
        ),
        in_specs=hbm_space * 5,
        out_specs=tuple(vmem(4)),
        scratch_shapes=[
            pltpu.VMEM((SLAB, BASES), jnp.int32),
            pltpu.VMEM((3, C), F32),
            pltpu.VMEM((5, 3, C), F32),
            pltpu.VMEM((SLAB, C), BF16),
            pltpu.SemaphoreType.DMA((7,)),
        ],
        compiler_params=pltpu.CompilerParams(vmem_limit_bytes=16 * 1024 * 1024),
        cost_estimate=pl.CostEstimate(
            flops=800_000_000, bytes_accessed=5_000_000, transcendentals=400_000
        ),
        name="inner",
    )(in_hbm(bases), in_hbm(embed_table), in_hbm(norm_gains), in_hbm(taps), in_hbm(point_weight))
    trunk, keys, queries, _, _ = pl.pallas_call(
        outer_kernel,
        out_shape=(
            jax.ShapeDtypeStruct((SLAB, C), BF16),
            jax.ShapeDtypeStruct((16, 16, PC), BF16),
            jax.ShapeDtypeStruct((32, PC), F32),
        )
        + state,
        in_specs=vmem(10),
        out_specs=tuple(vmem(5)),
        scratch_shapes=[pltpu.VMEM((288, C), BF16)],
        input_output_aliases={8: 3, 9: 4},
        compiler_params=pltpu.CompilerParams(vmem_limit_bytes=16 * 1024 * 1024),
        cost_estimate=pl.CostEstimate(
            flops=1_000_000_000, bytes_accessed=1_000_000, transcendentals=600_000
        ),
        name="outer",
    )(inner, outer, norm_gains, taps, table, point, query_weight, key_weight, x, n)

    own_keys = lax.all_to_all(keys, ("x_hi", "z"), 0, 0, tiled=False)
    other_keys = lax.ppermute(own_keys, "core", [(0, 1), (1, 0)])

    weights = pl.pallas_call(
        weights_kernel,
        out_shape=jax.ShapeDtypeStruct((8, 3 * PC, 2 * PC), BF16),
        in_specs=vmem(2),
        out_specs=vmem(1)[0],
        scratch_shapes=[pltpu.VMEM((18, PC, PC), BF16)],
        compiler_params=pltpu.CompilerParams(vmem_limit_bytes=8 * 1024 * 1024),
        cost_estimate=pl.CostEstimate(
            flops=400_000_000, bytes_accessed=2_000_000, transcendentals=0
        ),
        name="weights",
    )(queries, pair_kernel)
    pair_map = pl.pallas_call(
        pair_kernel_body,
        out_shape=jax.ShapeDtypeStruct((16, 512, PC), BF16),
        in_specs=vmem(4),
        out_specs=pl.BlockSpec(memory_space=pl.ANY),
        scratch_shapes=[
            pltpu.VMEM((512, 3 * PC), BF16),
            pltpu.VMEM((16, 512, PC), BF16),
            pltpu.SemaphoreType.DMA((8,)),
        ],
        compiler_params=pltpu.CompilerParams(vmem_limit_bytes=16 * 1024 * 1024),
        name="pair",
    )(queries, own_keys, other_keys, weights)
    return (trunk, pair_map)


def solution(mesh):
    devices = mesh.devices.reshape(2, 8, 2, -1)
    fine = Mesh(devices, ("x_hi", "z", "core", "batch"))
    rows = ("batch", "x_hi", "z", "core")
    return jax.shard_map(
        on_device,
        mesh=fine,
        in_specs=(P(rows, None), P(), P(), P(), P(), P(), P(), P()),
        out_specs=(P(rows, None), P(rows, None, None)),
        check_vma=False,
    )
```

```python
import math

import jax
import jax.numpy as jnp
from jax import lax
from jax.experimental import pallas as pl
from jax.experimental.pallas import tpu as pltpu
from jax.sharding import Mesh
from jax.sharding import PartitionSpec as P

F32 = jnp.float32
BF16 = jnp.bfloat16
C = 768
PC = 128
BASES = 128
BINS = 8192
SLAB = 256
POOL = 16
HALO = 112
ROWS = SLAB + 2 * HALO
DILATIONS = (2, 8, 32)
STEP = 16

GELU_A = math.sqrt(2.0 / math.pi)
GELU_B = 0.044715 * GELU_A


def gelu_of_half(half):
    half = half.astype(BF16)
    squared = half * half
    inner = half * (jnp.asarray(2.0 * GELU_A, BF16) + jnp.asarray(8.0 * GELU_B, BF16) * squared)
    return half + half * jnp.tanh(inner)


def spread_matrix():
    return (
        lax.broadcasted_iota(jnp.int32, (BASES, 4 * BASES), 1) // 4
        == lax.broadcasted_iota(jnp.int32, (BASES, 4 * BASES), 0)
    ).astype(F32).astype(BF16)


def one_hot_rows(codes, spread):
    repeated = jnp.dot(codes.astype(F32).astype(BF16), spread, preferred_element_type=F32)
    base = (lax.broadcasted_iota(jnp.int32, repeated.shape, 1) % 4).astype(F32)
    return jnp.where(repeated == base, 1.0, 0.0).astype(BF16)


def norm_rows(x_ref, n_ref, layer, start, stop, scale=None):
    for at in range(start, stop, STEP):
        rows = x_ref[at : at + STEP, :]
        mean = jnp.sum(rows * rows, axis=-1, keepdims=True) * (1.0 / C)
        factor = lax.rsqrt(mean + 1e-06)
        if scale is not None:
            factor = factor * scale
        rows = rows * factor
        for c in range(C // 128):
            n_ref[layer, c, at : at + STEP, :] = rows[:, c * 128 : (c + 1) * 128]


def spread_taps(taps, gains, wide_taps):
    for layer in range(3):
        gain = gains[layer : layer + 1, :] * 0.5
        for t in range(5):
            row = taps[t, layer : layer + 1, :] * gain
            wide_taps[layer, t] = jnp.broadcast_to(row, (8, C))


def conv_rows(n_ref, a_ref, layer, wide_taps, start, stop, to):
    reach = DILATIONS[layer]
    for at in range(start, stop, STEP):
        for c in range(C // 128):
            cols = slice(c * 128, (c + 1) * 128)
            halves = []
            for row in (at, at + 8):
                half = None
                for t in range(5):
                    low = row + (t - 2) * reach
                    term = n_ref[layer, c, low : low + 8, :] * wide_taps[layer, t, :, cols]
                    half = term if half is None else half + term
                halves.append(half)
            half = jnp.concatenate(halves, axis=0)
            a_ref[to + at - start : to + at - start + STEP, cols] = gelu_of_half(half)


def mix(a_ref, x_ref, weights, start, stop, at):
    for strip in range(3):
        cols = slice(strip * 256, strip * 256 + 256)
        update = jnp.dot(
            a_ref[at : at + stop - start, :], weights[:, cols], preferred_element_type=F32
        )
        x_ref[start:stop, cols] = x_ref[start:stop, cols] + update


def inner_kernel(
    own_hbm, table_hbm, gains_hbm, taps_hbm, point_hbm,
    x_ref, n_ref, table, point,
    own, gains, taps, wide_taps, a_ref, sems,
):
    moves = [(own_hbm, own), (table_hbm, table), (gains_hbm, gains), (taps_hbm, taps)]
    moves += [(point_hbm.at[layer], point.at[layer]) for layer in range(3)]
    copies = [
        pltpu.make_async_copy(source, target, sems.at[k])
        for k, (source, target) in enumerate(moves)
    ]
    for copy in copies:
        copy.start()
    spread = spread_matrix()
    copies[0].wait()
    for half in range(2):
        rows = slice(half * 128, half * 128 + 128)
        a_ref[rows, 0 : 4 * BASES] = one_hot_rows(own[rows, :], spread)
    copies[1].wait()
    x_ref[HALO : HALO + SLAB, :] = jnp.dot(
        a_ref[:, 0 : 4 * BASES], table[...], preferred_element_type=F32
    )
    copies[2].wait()
    copies[3].wait()
    spread_taps(taps, gains, wide_taps)
    norm_rows(x_ref, n_ref, 0, 112, 368)
    for layer, low, high in ((0, 128, 352), (1, 144, 336)):
        copies[4 + layer].wait()
        middle = (low + high) // 2
        for start, stop in ((low, middle), (middle, high)):
            conv_rows(n_ref, a_ref, layer, wide_taps, start, stop, start - low)
            mix(a_ref, x_ref, point.at[layer], start, stop, start - low)
            norm_rows(x_ref, n_ref, layer + 1, start, stop)
    copies[6].wait()


def outer_kernel(
    inner, outer, gains, taps, table, point, query_w, key_w, x_in, n_in,
    trunk_out, keys_out, query_out, x_ref, n_ref, wide_taps, a_ref,
):
    del x_in, n_in
    place = lax.axis_index(("x_hi", "z", "core"))
    core = lax.axis_index("core")
    low_bases = jnp.where(core == 0, outer[SLAB - HALO :, :], inner[SLAB - HALO :, :])
    high_bases = jnp.where(core == 0, inner[:HALO, :], outer[:HALO, :])
    spread = spread_matrix()
    a_ref[0:HALO, 0 : 4 * BASES] = one_hot_rows(low_bases, spread)
    a_ref[HALO : 2 * HALO, 0 : 4 * BASES] = one_hot_rows(high_bases, spread)
    x_ref[0:HALO, :] = jnp.dot(
        a_ref[0:HALO, 0 : 4 * BASES], table[...], preferred_element_type=F32
    )
    x_ref[HALO + SLAB :, :] = jnp.dot(
        a_ref[HALO : 2 * HALO, 0 : 4 * BASES], table[...], preferred_element_type=F32
    )
    spread_taps(taps, gains, wide_taps)
    low_scale = jnp.where(place == 0, 0.0, 1.0)
    high_scale = jnp.where(place == 31, 0.0, 1.0)

    norm_rows(x_ref, n_ref, 0, 0, 112, low_scale)
    norm_rows(x_ref, n_ref, 0, 368, 480, high_scale)
    for layer, reach_out in ((0, 0), (1, 16)):
        low, high = 16 + reach_out, 352 - reach_out
        conv_rows(n_ref, a_ref, layer, wide_taps, low, low + 112, 0)
        mix(a_ref, x_ref, point.at[layer], low, low + 112, 0)
        norm_rows(x_ref, n_ref, layer + 1, low, 112, low_scale)
        norm_rows(x_ref, n_ref, layer + 1, 112, low + 112)
        conv_rows(n_ref, a_ref, layer, wide_taps, high, high + 112, 112)
        mix(a_ref, x_ref, point.at[layer], high, high + 112, 112)
        norm_rows(x_ref, n_ref, layer + 1, high, 368)
        norm_rows(x_ref, n_ref, layer + 1, 368, high + 112, high_scale)
    for start, stop in ((96, 240), (240, 384)):
        conv_rows(n_ref, a_ref, 2, wide_taps, start, stop, start - 96)
        mix(a_ref, x_ref, point.at[2], start, stop, start - 96)

    trunk = x_ref[96:384, :].astype(BF16)
    trunk_out[...] = trunk[POOL : POOL + SLAB, :]
    pooling = jnp.where(
        lax.broadcasted_iota(jnp.int32, (32, 288), 1) // POOL
        == lax.broadcasted_iota(jnp.int32, (32, 288), 0),
        1.0 / POOL,
        0.0,
    ).astype(BF16)
    pooled = jnp.dot(pooling, trunk, preferred_element_type=F32).astype(BF16)
    queries = jnp.dot(pooled, query_w[...], preferred_element_type=F32).astype(BF16).astype(F32)
    keys = jnp.dot(pooled, key_w[...], preferred_element_type=F32)
    row = place * (SLAB // POOL) - 1 + lax.broadcasted_iota(jnp.int32, (32, PC), 0)
    query_out[...] = jnp.where((row >= 0) & (row < BINS // POOL), queries, 0.0)
    mine = pltpu.roll(keys, 31, 0)[0:16].astype(BF16)
    for peer in range(16):
        keys_out[peer] = mine


def weights_kernel(queries, kernel, weights, wide_q):
    flipped = jnp.transpose(queries[...], (1, 0)) * 0.5
    for i in range(18):
        wide_q[i] = jnp.broadcast_to(flipped[:, i : i + 1], (PC, PC)).astype(BF16)

    def two_rows(i, _):
        for r in range(2):
            row = 2 * i + r
            for b in range(3):
                mixed = wide_q[row] * kernel[0, b]
                mixed = mixed + wide_q[row + 1] * kernel[1, b]
                mixed = mixed + wide_q[row + 2] * kernel[2, b]
                weights[i, b * PC : (b + 1) * PC, r * PC : (r + 1) * PC] = mixed
        return 0

    lax.fori_loop(0, 8, two_rows, 0)


def pair_kernel_body(queries, own, other, weights, out_hbm, key_cat, key_f, out_ref, sems):
    core = lax.axis_index("core")
    for g in range(16):
        mine = own[g]
        theirs = other[g]
        key_cat[g * 32 : g * 32 + 16, PC : 2 * PC] = jnp.where(core == 0, mine, theirs)
        key_cat[g * 32 + 16 : g * 32 + 32, PC : 2 * PC] = jnp.where(core == 0, theirs, mine)
    keys = key_cat[:, PC : 2 * PC].astype(F32)
    key_f[...] = keys
    at = lax.broadcasted_iota(jnp.int32, keys.shape, 0)
    before = jnp.where(at == 0, 0.0, pltpu.roll(keys, 1, 0))
    after = jnp.where(at == 511, 0.0, pltpu.roll(keys, 511, 0))
    key_cat[:, 0:PC] = before.astype(BF16)
    key_cat[:, 2 * PC : 3 * PC] = after.astype(BF16)

    def copy_of(i):
        return pltpu.make_async_copy(
            out_ref.at[pl.ds(2 * i, 2)], out_hbm.at[pl.ds(2 * i, 2)], sems.at[i]
        )

    for i in range(8):
        query_rows = [queries[2 * i + r + 1 : 2 * i + r + 2, :].astype(BF16) for r in range(2)]
        for m in range(2):
            rows = slice(m * 256, m * 256 + 256)
            half = jnp.dot(key_cat[rows, :], weights[i], preferred_element_type=F32)
            key = key_f[rows, :].astype(BF16)
            for r in range(2):
                gelu = gelu_of_half(half[:, r * PC : (r + 1) * PC])
                out_ref[2 * i + r, rows, :] = key * query_rows[r] + gelu
        copy_of(i).start()

    def finish(i, _):
        copy_of(i).wait()
        return 0

    lax.fori_loop(0, 8, finish, 0)


def in_hbm(array):
    return pltpu.with_memory_space_constraint(array, pltpu.HBM)


def vmem(count):
    return [pl.BlockSpec(memory_space=pltpu.VMEM)] * count


def on_device(
    bases, embed_table, norm_gains, depth_taps, point_weight, query_weight, key_weight, pair_kernel
):
    seq = ("x_hi", "z", "core")
    outer_pairs = []
    for i in range(1, 31, 2):
        outer_pairs += [(i, i + 1), (i + 1, i)]
    inner = lax.ppermute(bases, "core", [(0, 1), (1, 0)])
    outer = lax.ppermute(bases, seq, outer_pairs)

    taps = jnp.transpose(depth_taps, (1, 0, 2))
    hbm_space = [pl.BlockSpec(memory_space=pltpu.HBM)]
    state = (
        jax.ShapeDtypeStruct((ROWS, C), F32),
        jax.ShapeDtypeStruct((3, C // 128, ROWS, 128), F32),
    )
    x, n, table, point = pl.pallas_call(
        inner_kernel,
        out_shape=state
        + (
            jax.ShapeDtypeStruct((4 * BASES, C), BF16),
            jax.ShapeDtypeStruct((3, C, C), BF16),
        ),
        in_specs=hbm_space * 5,
        out_specs=tuple(vmem(4)),
        scratch_shapes=[
            pltpu.VMEM((SLAB, BASES), jnp.int32),
            pltpu.VMEM((3, C), F32),
            pltpu.VMEM((5, 3, C), F32),
            pltpu.VMEM((3, 5, 8, C), F32),
            pltpu.VMEM((SLAB, C), BF16),
            pltpu.SemaphoreType.DMA((7,)),
        ],
        compiler_params=pltpu.CompilerParams(vmem_limit_bytes=16 * 1024 * 1024),
        cost_estimate=pl.CostEstimate(
            flops=800_000_000, bytes_accessed=5_000_000, transcendentals=400_000
        ),
        name="inner",
    )(in_hbm(bases), in_hbm(embed_table), in_hbm(norm_gains), in_hbm(taps), in_hbm(point_weight))
    trunk, keys, queries, _, _ = pl.pallas_call(
        outer_kernel,
        out_shape=(
            jax.ShapeDtypeStruct((SLAB, C), BF16),
            jax.ShapeDtypeStruct((16, 16, PC), BF16),
            jax.ShapeDtypeStruct((32, PC), F32),
        )
        + state,
        in_specs=vmem(10),
        out_specs=tuple(vmem(5)),
        scratch_shapes=[pltpu.VMEM((3, 5, 8, C), F32), pltpu.VMEM((288, C), BF16)],
        input_output_aliases={8: 3, 9: 4},
        compiler_params=pltpu.CompilerParams(vmem_limit_bytes=16 * 1024 * 1024),
        cost_estimate=pl.CostEstimate(
            flops=1_000_000_000, bytes_accessed=1_000_000, transcendentals=600_000
        ),
        name="outer",
    )(inner, outer, norm_gains, taps, table, point, query_weight, key_weight, x, n)

    own_keys = lax.all_to_all(keys, ("x_hi", "z"), 0, 0, tiled=False)
    other_keys = lax.ppermute(own_keys, "core", [(0, 1), (1, 0)])

    weights = pl.pallas_call(
        weights_kernel,
        out_shape=jax.ShapeDtypeStruct((8, 3 * PC, 2 * PC), BF16),
        in_specs=vmem(2),
        out_specs=vmem(1)[0],
        scratch_shapes=[pltpu.VMEM((18, PC, PC), BF16)],
        compiler_params=pltpu.CompilerParams(vmem_limit_bytes=8 * 1024 * 1024),
        cost_estimate=pl.CostEstimate(
            flops=400_000_000, bytes_accessed=2_000_000, transcendentals=0
        ),
        name="weights",
    )(queries, pair_kernel)
    pair_map = pl.pallas_call(
        pair_kernel_body,
        out_shape=jax.ShapeDtypeStruct((16, 512, PC), BF16),
        in_specs=vmem(4),
        out_specs=pl.BlockSpec(memory_space=pl.ANY),
        scratch_shapes=[
            pltpu.VMEM((512, 3 * PC), BF16),
            pltpu.VMEM((512, PC), F32),
            pltpu.VMEM((16, 512, PC), BF16),
            pltpu.SemaphoreType.DMA((8,)),
        ],
        compiler_params=pltpu.CompilerParams(vmem_limit_bytes=16 * 1024 * 1024),
        name="pair",
    )(queries, own_keys, other_keys, weights)
    return (trunk, pair_map)


def solution(mesh):
    devices = mesh.devices.reshape(2, 8, 2, -1)
    fine = Mesh(devices, ("x_hi", "z", "core", "batch"))
    rows = ("batch", "x_hi", "z", "core")
    return jax.shard_map(
        on_device,
        mesh=fine,
        in_specs=(P(rows, None), P(), P(), P(), P(), P(), P(), P()),
        out_specs=(P(rows, None), P(rows, None, None)),
        check_vma=False,
    )
```

```python
import math

import jax
import jax.numpy as jnp
from jax import lax
from jax.experimental import pallas as pl
from jax.experimental.pallas import tpu as pltpu
from jax.sharding import Mesh
from jax.sharding import PartitionSpec as P

F32 = jnp.float32
BF16 = jnp.bfloat16
C = 768
PC = 128
BASES = 128
BINS = 8192
SLAB = 256
POOL = 16
HALO = 112
ROWS = SLAB + 2 * HALO
DILATIONS = (2, 8, 32)
STEP = 16

GELU_A = math.sqrt(2.0 / math.pi)
GELU_B = 0.044715 * GELU_A


def gelu_of_half(half):
    half = half.astype(BF16)
    squared = half * half
    inner = half * (jnp.asarray(2.0 * GELU_A, BF16) + jnp.asarray(8.0 * GELU_B, BF16) * squared)
    return half + half * jnp.tanh(inner)


def spread_matrix():
    return (
        lax.broadcasted_iota(jnp.int32, (BASES, 4 * BASES), 1) // 4
        == lax.broadcasted_iota(jnp.int32, (BASES, 4 * BASES), 0)
    ).astype(F32).astype(BF16)


def one_hot_rows(codes, spread):
    repeated = jnp.dot(codes, spread, preferred_element_type=F32)
    base = (lax.broadcasted_iota(jnp.int32, repeated.shape, 1) % 4).astype(F32)
    return jnp.where(repeated == base, 1.0, 0.0).astype(BF16)


def norm_rows(x_ref, n_ref, layer, start, stop, scale=None):
    for at in range(start, stop, STEP):
        rows = x_ref[at : at + STEP, :]
        mean = jnp.sum(rows * rows, axis=-1, keepdims=True) * (1.0 / C)
        factor = lax.rsqrt(mean + 1e-06)
        if scale is not None:
            factor = factor * scale
        rows = rows * factor
        for c in range(C // 128):
            n_ref[layer, c, at : at + STEP, :] = rows[:, c * 128 : (c + 1) * 128]


def spread_taps(taps, gains, wide_taps):
    for layer in range(3):
        gain = gains[layer : layer + 1, :] * 0.5
        for t in range(5):
            row = taps[t, layer : layer + 1, :] * gain
            wide_taps[layer, t] = jnp.broadcast_to(row, (8, C))


def conv_rows(n_ref, a_ref, layer, wide_taps, start, stop, to):
    reach = DILATIONS[layer]
    for at in range(start, stop, STEP):
        for c in range(C // 128):
            cols = slice(c * 128, (c + 1) * 128)
            halves = []
            for row in (at, at + 8):
                half = None
                for t in range(5):
                    low = row + (t - 2) * reach
                    term = n_ref[layer, c, low : low + 8, :] * wide_taps[layer, t, :, cols]
                    half = term if half is None else half + term
                halves.append(half)
            half = jnp.concatenate(halves, axis=0)
            a_ref[to + at - start : to + at - start + STEP, cols] = gelu_of_half(half)


def mix(a_ref, x_ref, weights, start, stop, at):
    for strip in range(3):
        cols = slice(strip * 256, strip * 256 + 256)
        update = jnp.dot(
            a_ref[at : at + stop - start, :], weights[:, cols], preferred_element_type=F32
        )
        x_ref[start:stop, cols] = x_ref[start:stop, cols] + update


def inner_kernel(
    own_hbm, table_hbm, gains_hbm, taps_hbm, point_hbm,
    x_ref, n_ref, table, point,
    own, gains, taps, wide_taps, a_ref, sems,
):
    moves = [(own_hbm, own), (table_hbm, table), (gains_hbm, gains), (taps_hbm, taps)]
    moves += [(point_hbm.at[layer], point.at[layer]) for layer in range(3)]
    copies = [
        pltpu.make_async_copy(source, target, sems.at[k])
        for k, (source, target) in enumerate(moves)
    ]
    for copy in copies:
        copy.start()
    spread = spread_matrix()
    copies[0].wait()
    for half in range(2):
        rows = slice(half * 128, half * 128 + 128)
        a_ref[rows, 0 : 4 * BASES] = one_hot_rows(own[rows, :].astype(F32).astype(BF16), spread)
    copies[1].wait()
    x_ref[HALO : HALO + SLAB, :] = jnp.dot(
        a_ref[:, 0 : 4 * BASES], table[...], preferred_element_type=F32
    )
    copies[2].wait()
    copies[3].wait()
    spread_taps(taps, gains, wide_taps)
    norm_rows(x_ref, n_ref, 0, 112, 368)
    for layer, low, high in ((0, 128, 352), (1, 144, 336)):
        copies[4 + layer].wait()
        middle = (low + high) // 2
        for start, stop in ((low, middle), (middle, high)):
            conv_rows(n_ref, a_ref, layer, wide_taps, start, stop, start - low)
            mix(a_ref, x_ref, point.at[layer], start, stop, start - low)
            norm_rows(x_ref, n_ref, layer + 1, start, stop)
    copies[6].wait()


def outer_kernel(
    inner, outer, gains, taps, table, point, query_w, key_w, x_in, n_in,
    trunk_out, keys_out, query_out, x_ref, n_ref, wide_taps, a_ref,
):
    del x_in, n_in
    place = lax.axis_index(("x_hi", "z", "core"))
    core = lax.axis_index("core")
    low_bases = jnp.where(core == 0, outer[...], inner[...])
    high_bases = jnp.where(core == 0, inner[...], outer[...])
    spread = spread_matrix()
    a_ref[0:HALO, 0 : 4 * BASES] = one_hot_rows(low_bases, spread)
    a_ref[HALO : 2 * HALO, 0 : 4 * BASES] = one_hot_rows(high_bases, spread)
    x_ref[0:HALO, :] = jnp.dot(
        a_ref[0:HALO, 0 : 4 * BASES], table[...], preferred_element_type=F32
    )
    x_ref[HALO + SLAB :, :] = jnp.dot(
        a_ref[HALO : 2 * HALO, 0 : 4 * BASES], table[...], preferred_element_type=F32
    )
    spread_taps(taps, gains, wide_taps)
    low_scale = jnp.where(place == 0, 0.0, 1.0)
    high_scale = jnp.where(place == 31, 0.0, 1.0)

    norm_rows(x_ref, n_ref, 0, 0, 112, low_scale)
    norm_rows(x_ref, n_ref, 0, 368, 480, high_scale)
    for layer, reach_out in ((0, 0), (1, 16)):
        low, high = 16 + reach_out, 352 - reach_out
        conv_rows(n_ref, a_ref, layer, wide_taps, low, low + 112, 0)
        mix(a_ref, x_ref, point.at[layer], low, low + 112, 0)
        norm_rows(x_ref, n_ref, layer + 1, low, 112, low_scale)
        norm_rows(x_ref, n_ref, layer + 1, 112, low + 112)
        conv_rows(n_ref, a_ref, layer, wide_taps, high, high + 112, 112)
        mix(a_ref, x_ref, point.at[layer], high, high + 112, 112)
        norm_rows(x_ref, n_ref, layer + 1, high, 368)
        norm_rows(x_ref, n_ref, layer + 1, 368, high + 112, high_scale)
    for start, stop in ((96, 240), (240, 384)):
        conv_rows(n_ref, a_ref, 2, wide_taps, start, stop, start - 96)
        mix(a_ref, x_ref, point.at[2], start, stop, start - 96)

    trunk = x_ref[96:384, :].astype(BF16)
    trunk_out[...] = trunk[POOL : POOL + SLAB, :]
    pooling = jnp.where(
        lax.broadcasted_iota(jnp.int32, (32, 288), 1) // POOL
        == lax.broadcasted_iota(jnp.int32, (32, 288), 0),
        1.0 / POOL,
        0.0,
    ).astype(BF16)
    pooled = jnp.dot(pooling, trunk, preferred_element_type=F32).astype(BF16)
    queries = jnp.dot(pooled, query_w[...], preferred_element_type=F32).astype(BF16).astype(F32)
    keys = jnp.dot(pooled, key_w[...], preferred_element_type=F32)
    row = place * (SLAB // POOL) - 1 + lax.broadcasted_iota(jnp.int32, (32, PC), 0)
    query_out[...] = jnp.where((row >= 0) & (row < BINS // POOL), queries, 0.0)
    mine = pltpu.roll(keys, 31, 0)[0:16].astype(BF16)
    for peer in range(16):
        keys_out[peer] = mine


def weights_kernel(queries, kernel, trunk, weights, trunk_hbm, wide_q, sem):
    copy = pltpu.make_async_copy(trunk, trunk_hbm, sem)
    copy.start()
    flipped = jnp.transpose(queries[...], (1, 0)) * 0.5
    for i in range(18):
        wide_q[i] = jnp.broadcast_to(flipped[:, i : i + 1], (PC, PC)).astype(BF16)

    def two_rows(i, _):
        for r in range(2):
            row = 2 * i + r
            for b in range(3):
                mixed = wide_q[row] * kernel[0, b]
                mixed = mixed + wide_q[row + 1] * kernel[1, b]
                mixed = mixed + wide_q[row + 2] * kernel[2, b]
                weights[i, b * PC : (b + 1) * PC, r * PC : (r + 1) * PC] = mixed
        return 0

    lax.fori_loop(0, 8, two_rows, 0)
    copy.wait()


def pair_kernel_body(queries, own, other, weights, out_hbm, key_cat, key_f, out_ref, sems):
    core = lax.axis_index("core")
    for g in range(16):
        mine = own[g]
        theirs = other[g]
        key_cat[g * 32 : g * 32 + 16, PC : 2 * PC] = jnp.where(core == 0, mine, theirs)
        key_cat[g * 32 + 16 : g * 32 + 32, PC : 2 * PC] = jnp.where(core == 0, theirs, mine)
    keys = key_cat[:, PC : 2 * PC].astype(F32)
    key_f[...] = keys
    at = lax.broadcasted_iota(jnp.int32, keys.shape, 0)
    before = jnp.where(at == 0, 0.0, pltpu.roll(keys, 1, 0))
    after = jnp.where(at == 511, 0.0, pltpu.roll(keys, 511, 0))
    key_cat[:, 0:PC] = before.astype(BF16)
    key_cat[:, 2 * PC : 3 * PC] = after.astype(BF16)

    def copy_of(i):
        return pltpu.make_async_copy(
            out_ref.at[pl.ds(2 * i, 2)], out_hbm.at[pl.ds(2 * i, 2)], sems.at[i]
        )

    for i in range(8):
        query_rows = [queries[2 * i + r + 1 : 2 * i + r + 2, :].astype(BF16) for r in range(2)]
        for m in range(2):
            rows = slice(m * 256, m * 256 + 256)
            half = jnp.dot(key_cat[rows, :], weights[i], preferred_element_type=F32)
            key = key_f[rows, :].astype(BF16)
            for r in range(2):
                gelu = gelu_of_half(half[:, r * PC : (r + 1) * PC])
                out_ref[2 * i + r, rows, :] = key * query_rows[r] + gelu
        copy_of(i).start()

    def finish(i, _):
        copy_of(i).wait()
        return 0

    lax.fori_loop(0, 8, finish, 0)


def in_hbm(array):
    return pltpu.with_memory_space_constraint(array, pltpu.HBM)


def vmem(count):
    return [pl.BlockSpec(memory_space=pltpu.VMEM)] * count


def on_device(
    bases, embed_table, norm_gains, depth_taps, point_weight, query_weight, key_weight, pair_kernel
):
    core = lax.axis_index("core")
    seq = ("x_hi", "z", "core")
    outer_pairs = []
    for i in range(1, 31, 2):
        outer_pairs += [(i, i + 1), (i + 1, i)]
    toward_core = jnp.where(core == 0, SLAB - HALO, 0)
    ends = [
        lax.dynamic_slice(bases, (start, 0), (HALO, BASES)).astype(BF16)
        for start in (toward_core, SLAB - HALO - toward_core)
    ]
    inner = lax.ppermute(ends[0], "core", [(0, 1), (1, 0)])
    outer = lax.ppermute(ends[1], seq, outer_pairs)

    taps = jnp.transpose(depth_taps, (1, 0, 2))
    hbm_space = [pl.BlockSpec(memory_space=pltpu.HBM)]
    state = (
        jax.ShapeDtypeStruct((ROWS, C), F32),
        jax.ShapeDtypeStruct((3, C // 128, ROWS, 128), F32),
    )
    x, n, table, point = pl.pallas_call(
        inner_kernel,
        out_shape=state
        + (
            jax.ShapeDtypeStruct((4 * BASES, C), BF16),
            jax.ShapeDtypeStruct((3, C, C), BF16),
        ),
        in_specs=hbm_space * 5,
        out_specs=tuple(vmem(4)),
        scratch_shapes=[
            pltpu.VMEM((SLAB, BASES), jnp.int32),
            pltpu.VMEM((3, C), F32),
            pltpu.VMEM((5, 3, C), F32),
            pltpu.VMEM((3, 5, 8, C), F32),
            pltpu.VMEM((SLAB, C), BF16),
            pltpu.SemaphoreType.DMA((7,)),
        ],
        compiler_params=pltpu.CompilerParams(vmem_limit_bytes=16 * 1024 * 1024),
        cost_estimate=pl.CostEstimate(
            flops=800_000_000, bytes_accessed=5_000_000, transcendentals=400_000
        ),
        name="inner",
    )(in_hbm(bases), in_hbm(embed_table), in_hbm(norm_gains), in_hbm(taps), in_hbm(point_weight))
    trunk, keys, queries, _, _ = pl.pallas_call(
        outer_kernel,
        out_shape=(
            jax.ShapeDtypeStruct((SLAB, C), BF16),
            jax.ShapeDtypeStruct((16, 16, PC), BF16),
            jax.ShapeDtypeStruct((32, PC), F32),
        )
        + state,
        in_specs=vmem(10),
        out_specs=tuple(vmem(5)),
        scratch_shapes=[pltpu.VMEM((3, 5, 8, C), F32), pltpu.VMEM((288, C), BF16)],
        input_output_aliases={8: 3, 9: 4},
        compiler_params=pltpu.CompilerParams(vmem_limit_bytes=16 * 1024 * 1024),
        cost_estimate=pl.CostEstimate(
            flops=1_000_000_000, bytes_accessed=1_000_000, transcendentals=600_000
        ),
        name="outer",
    )(inner, outer, norm_gains, taps, table, point, query_weight, key_weight, x, n)

    own_keys = lax.all_to_all(keys, ("x_hi", "z"), 0, 0, tiled=False)
    other_keys = lax.ppermute(own_keys, "core", [(0, 1), (1, 0)])

    weights, trunk = pl.pallas_call(
        weights_kernel,
        out_shape=(
            jax.ShapeDtypeStruct((8, 3 * PC, 2 * PC), BF16),
            jax.ShapeDtypeStruct((SLAB, C), BF16),
        ),
        in_specs=vmem(3),
        out_specs=(vmem(1)[0], pl.BlockSpec(memory_space=pl.ANY)),
        scratch_shapes=[pltpu.VMEM((18, PC, PC), BF16), pltpu.SemaphoreType.DMA],
        compiler_params=pltpu.CompilerParams(vmem_limit_bytes=8 * 1024 * 1024),
        cost_estimate=pl.CostEstimate(
            flops=400_000_000, bytes_accessed=2_000_000, transcendentals=0
        ),
        name="weights",
    )(queries, pair_kernel, trunk)
    pair_map = pl.pallas_call(
        pair_kernel_body,
        out_shape=jax.ShapeDtypeStruct((16, 512, PC), BF16),
        in_specs=vmem(4),
        out_specs=pl.BlockSpec(memory_space=pl.ANY),
        scratch_shapes=[
            pltpu.VMEM((512, 3 * PC), BF16),
            pltpu.VMEM((512, PC), F32),
            pltpu.VMEM((16, 512, PC), BF16),
            pltpu.SemaphoreType.DMA((8,)),
        ],
        compiler_params=pltpu.CompilerParams(vmem_limit_bytes=16 * 1024 * 1024),
        name="pair",
    )(queries, own_keys, other_keys, weights)
    return (trunk, pair_map)


def solution(mesh):
    devices = mesh.devices.reshape(2, 8, 2, -1)
    fine = Mesh(devices, ("x_hi", "z", "core", "batch"))
    rows = ("batch", "x_hi", "z", "core")
    return jax.shard_map(
        on_device,
        mesh=fine,
        in_specs=(P(rows, None), P(), P(), P(), P(), P(), P(), P()),
        out_specs=(P(rows, None), P(rows, None, None)),
        check_vma=False,
    )
```

```python
import math

import jax
import jax.numpy as jnp
from jax import lax
from jax.experimental import pallas as pl
from jax.experimental.pallas import tpu as pltpu
from jax.sharding import Mesh
from jax.sharding import PartitionSpec as P

F32 = jnp.float32
BF16 = jnp.bfloat16
C = 768
PC = 128
BASES = 128
BINS = 8192
SLAB = 256
POOL = 16
HALO = 112
ROWS = SLAB + 2 * HALO
DILATIONS = (2, 8, 32)
STEP = 16

GELU_A = math.sqrt(2.0 / math.pi)
GELU_B = 0.044715 * GELU_A


def gelu_of_half(half):
    half = half.astype(BF16)
    squared = half * half
    inner = half * (jnp.asarray(2.0 * GELU_A, BF16) + jnp.asarray(8.0 * GELU_B, BF16) * squared)
    return half + half * jnp.tanh(inner)


def spread_matrix():
    return (
        lax.broadcasted_iota(jnp.int32, (BASES, 4 * BASES), 1) // 4
        == lax.broadcasted_iota(jnp.int32, (BASES, 4 * BASES), 0)
    ).astype(F32).astype(BF16)


def one_hot_rows(codes, spread):
    repeated = jnp.dot(codes, spread, preferred_element_type=F32)
    base = (lax.broadcasted_iota(jnp.int32, repeated.shape, 1) % 4).astype(F32)
    return jnp.where(repeated == base, 1.0, 0.0).astype(BF16)


def norm_rows(x_ref, n_ref, layer, start, stop, scale=None):
    for at in range(start, stop, STEP):
        rows = x_ref[at : at + STEP, :]
        mean = jnp.sum(rows * rows, axis=-1, keepdims=True) * (1.0 / C)
        factor = lax.rsqrt(mean + 1e-06)
        if scale is not None:
            factor = factor * scale
        rows = rows * factor
        for c in range(C // 128):
            n_ref[layer, c, at : at + STEP, :] = rows[:, c * 128 : (c + 1) * 128]


def spread_taps(taps, gains, wide_taps):
    for layer in range(3):
        gain = gains[layer : layer + 1, :] * 0.5
        for t in range(5):
            row = taps[t, layer : layer + 1, :] * gain
            wide_taps[layer, t] = jnp.broadcast_to(row, (8, C))


def conv_rows(n_ref, a_ref, layer, wide_taps, start, stop, to):
    reach = DILATIONS[layer]
    for at in range(start, stop, STEP):
        for c in range(C // 128):
            cols = slice(c * 128, (c + 1) * 128)
            halves = []
            for row in (at, at + 8):
                half = None
                for t in range(5):
                    low = row + (t - 2) * reach
                    term = n_ref[layer, c, low : low + 8, :] * wide_taps[layer, t, :, cols]
                    half = term if half is None else half + term
                halves.append(half)
            half = jnp.concatenate(halves, axis=0)
            a_ref[to + at - start : to + at - start + STEP, cols] = gelu_of_half(half)


def mix(a_ref, x_ref, weights, start, stop, at):
    for strip in range(3):
        cols = slice(strip * 256, strip * 256 + 256)
        update = jnp.dot(
            a_ref[at : at + stop - start, :], weights[:, cols], preferred_element_type=F32
        )
        x_ref[start:stop, cols] = x_ref[start:stop, cols] + update


def ends_kernel(bases_hbm, to_core, to_chip, codes, spread, own, sem):
    copy = pltpu.make_async_copy(bases_hbm, own, sem)
    copy.start()
    spread[...] = spread_matrix()
    core = lax.axis_index("core")
    copy.wait()
    rows = own[...].astype(F32)
    head = rows[:HALO].astype(BF16)
    tail = rows[SLAB - HALO :].astype(BF16)
    to_core[...] = jnp.where(core == 0, tail, head)
    to_chip[...] = jnp.where(core == 0, head, tail)
    codes[...] = rows.astype(BF16)


def inner_kernel(codes, spread, table, gains, taps, point, x_ref, n_ref, wide_taps, a_ref):
    one_hot = one_hot_rows(codes[...], spread[...])
    x_ref[HALO : HALO + SLAB, :] = jnp.dot(one_hot, table[...], preferred_element_type=F32)
    spread_taps(taps, gains, wide_taps)
    norm_rows(x_ref, n_ref, 0, 112, 368)
    for layer, low, high in ((0, 128, 352), (1, 144, 336)):
        middle = (low + high) // 2
        for start, stop in ((low, middle), (middle, high)):
            conv_rows(n_ref, a_ref, layer, wide_taps, start, stop, start - low)
            mix(a_ref, x_ref, point.at[layer], start, stop, start - low)
            norm_rows(x_ref, n_ref, layer + 1, start, stop)


def outer_kernel(
    inner, outer, spread, gains, taps, table, point, query_w, key_w, x_in, n_in,
    trunk_out, keys_out, query_out, x_ref, n_ref, wide_taps, a_ref,
):
    del x_in, n_in
    place = lax.axis_index(("x_hi", "z", "core"))
    core = lax.axis_index("core")
    low_bases = jnp.where(core == 0, outer[...], inner[...])
    high_bases = jnp.where(core == 0, inner[...], outer[...])
    a_ref[0:HALO, 0 : 4 * BASES] = one_hot_rows(low_bases, spread[...])
    a_ref[HALO : 2 * HALO, 0 : 4 * BASES] = one_hot_rows(high_bases, spread[...])
    x_ref[0:HALO, :] = jnp.dot(
        a_ref[0:HALO, 0 : 4 * BASES], table[...], preferred_element_type=F32
    )
    x_ref[HALO + SLAB :, :] = jnp.dot(
        a_ref[HALO : 2 * HALO, 0 : 4 * BASES], table[...], preferred_element_type=F32
    )
    spread_taps(taps, gains, wide_taps)
    low_scale = jnp.where(place == 0, 0.0, 1.0)
    high_scale = jnp.where(place == 31, 0.0, 1.0)

    norm_rows(x_ref, n_ref, 0, 0, 112, low_scale)
    norm_rows(x_ref, n_ref, 0, 368, 480, high_scale)
    for layer, reach_out in ((0, 0), (1, 16)):
        low, high = 16 + reach_out, 352 - reach_out
        conv_rows(n_ref, a_ref, layer, wide_taps, low, low + 112, 0)
        mix(a_ref, x_ref, point.at[layer], low, low + 112, 0)
        norm_rows(x_ref, n_ref, layer + 1, low, 112, low_scale)
        norm_rows(x_ref, n_ref, layer + 1, 112, low + 112)
        conv_rows(n_ref, a_ref, layer, wide_taps, high, high + 112, 112)
        mix(a_ref, x_ref, point.at[layer], high, high + 112, 112)
        norm_rows(x_ref, n_ref, layer + 1, high, 368)
        norm_rows(x_ref, n_ref, layer + 1, 368, high + 112, high_scale)
    for start, stop in ((96, 240), (240, 384)):
        conv_rows(n_ref, a_ref, 2, wide_taps, start, stop, start - 96)
        mix(a_ref, x_ref, point.at[2], start, stop, start - 96)

    trunk = x_ref[96:384, :].astype(BF16)
    trunk_out[...] = trunk[POOL : POOL + SLAB, :]
    pooling = jnp.where(
        lax.broadcasted_iota(jnp.int32, (32, 288), 1) // POOL
        == lax.broadcasted_iota(jnp.int32, (32, 288), 0),
        1.0 / POOL,
        0.0,
    ).astype(BF16)
    pooled = jnp.dot(pooling, trunk, preferred_element_type=F32).astype(BF16)
    queries = jnp.dot(pooled, query_w[...], preferred_element_type=F32).astype(BF16).astype(F32)
    keys = jnp.dot(pooled, key_w[...], preferred_element_type=F32)
    row = place * (SLAB // POOL) - 1 + lax.broadcasted_iota(jnp.int32, (32, PC), 0)
    query_out[...] = jnp.where((row >= 0) & (row < BINS // POOL), queries, 0.0)
    mine = pltpu.roll(keys, 31, 0)[0:16].astype(BF16)
    for peer in range(16):
        keys_out[peer] = mine


def weights_kernel(queries, kernel, trunk, weights, trunk_hbm, wide_q, sem):
    copy = pltpu.make_async_copy(trunk, trunk_hbm, sem)
    copy.start()
    flipped = jnp.transpose(queries[...], (1, 0)) * 0.5
    for i in range(18):
        wide_q[i] = jnp.broadcast_to(flipped[:, i : i + 1], (PC, PC)).astype(BF16)

    def two_rows(i, _):
        for r in range(2):
            row = 2 * i + r
            for b in range(3):
                mixed = wide_q[row] * kernel[0, b]
                mixed = mixed + wide_q[row + 1] * kernel[1, b]
                mixed = mixed + wide_q[row + 2] * kernel[2, b]
                weights[i, b * PC : (b + 1) * PC, r * PC : (r + 1) * PC] = mixed
        return 0

    lax.fori_loop(0, 8, two_rows, 0)
    copy.wait()


def pair_kernel_body(queries, own, other, weights, out_hbm, key_cat, key_f, out_ref, sems):
    core = lax.axis_index("core")
    for g in range(16):
        mine = own[g]
        theirs = other[g]
        key_cat[g * 32 : g * 32 + 16, PC : 2 * PC] = jnp.where(core == 0, mine, theirs)
        key_cat[g * 32 + 16 : g * 32 + 32, PC : 2 * PC] = jnp.where(core == 0, theirs, mine)
    keys = key_cat[:, PC : 2 * PC].astype(F32)
    key_f[...] = keys
    at = lax.broadcasted_iota(jnp.int32, keys.shape, 0)
    before = jnp.where(at == 0, 0.0, pltpu.roll(keys, 1, 0))
    after = jnp.where(at == 511, 0.0, pltpu.roll(keys, 511, 0))
    key_cat[:, 0:PC] = before.astype(BF16)
    key_cat[:, 2 * PC : 3 * PC] = after.astype(BF16)

    def copy_of(i):
        return pltpu.make_async_copy(
            out_ref.at[pl.ds(2 * i, 2)], out_hbm.at[pl.ds(2 * i, 2)], sems.at[i]
        )

    for i in range(8):
        query_rows = [queries[2 * i + r + 1 : 2 * i + r + 2, :].astype(BF16) for r in range(2)]
        for m in range(2):
            rows = slice(m * 256, m * 256 + 256)
            half = jnp.dot(key_cat[rows, :], weights[i], preferred_element_type=F32)
            key = key_f[rows, :].astype(BF16)
            for r in range(2):
                gelu = gelu_of_half(half[:, r * PC : (r + 1) * PC])
                out_ref[2 * i + r, rows, :] = key * query_rows[r] + gelu
        copy_of(i).start()

    def finish(i, _):
        copy_of(i).wait()
        return 0

    lax.fori_loop(0, 8, finish, 0)


def in_hbm(array):
    return pltpu.with_memory_space_constraint(array, pltpu.HBM)


def vmem(count):
    return [pl.BlockSpec(memory_space=pltpu.VMEM)] * count


def on_device(
    bases, embed_table, norm_gains, depth_taps, point_weight, query_weight, key_weight, pair_kernel
):
    seq = ("x_hi", "z", "core")
    outer_pairs = []
    for i in range(1, 31, 2):
        outer_pairs += [(i, i + 1), (i + 1, i)]
    to_core, to_chip, codes, spread = pl.pallas_call(
        ends_kernel,
        out_shape=(
            jax.ShapeDtypeStruct((HALO, BASES), BF16),
            jax.ShapeDtypeStruct((HALO, BASES), BF16),
            jax.ShapeDtypeStruct((SLAB, BASES), BF16),
            jax.ShapeDtypeStruct((BASES, 4 * BASES), BF16),
        ),
        in_specs=[pl.BlockSpec(memory_space=pltpu.HBM)],
        out_specs=tuple(vmem(4)),
        scratch_shapes=[pltpu.VMEM((SLAB, BASES), jnp.int32), pltpu.SemaphoreType.DMA],
        compiler_params=pltpu.CompilerParams(vmem_limit_bytes=4 * 1024 * 1024),
        cost_estimate=pl.CostEstimate(
            flops=20_000_000_000, bytes_accessed=1_000_000, transcendentals=0
        ),
        name="ends",
    )(in_hbm(bases))
    inner = lax.ppermute(to_core, "core", [(0, 1), (1, 0)])
    outer = lax.ppermute(to_chip, seq, outer_pairs)

    taps = jnp.transpose(depth_taps, (1, 0, 2))
    state = (
        jax.ShapeDtypeStruct((ROWS, C), F32),
        jax.ShapeDtypeStruct((3, C // 128, ROWS, 128), F32),
    )
    x, n = pl.pallas_call(
        inner_kernel,
        out_shape=state,
        in_specs=vmem(6),
        out_specs=tuple(vmem(2)),
        scratch_shapes=[pltpu.VMEM((3, 5, 8, C), F32), pltpu.VMEM((SLAB, C), BF16)],
        compiler_params=pltpu.CompilerParams(vmem_limit_bytes=12 * 1024 * 1024),
        cost_estimate=pl.CostEstimate(
            flops=800_000_000, bytes_accessed=5_000_000, transcendentals=400_000
        ),
        name="inner",
    )(codes, spread, embed_table, norm_gains, taps, point_weight)
    trunk, keys, queries, _, _ = pl.pallas_call(
        outer_kernel,
        out_shape=(
            jax.ShapeDtypeStruct((SLAB, C), BF16),
            jax.ShapeDtypeStruct((16, 16, PC), BF16),
            jax.ShapeDtypeStruct((32, PC), F32),
        )
        + state,
        in_specs=vmem(11),
        out_specs=tuple(vmem(5)),
        scratch_shapes=[pltpu.VMEM((3, 5, 8, C), F32), pltpu.VMEM((288, C), BF16)],
        input_output_aliases={9: 3, 10: 4},
        compiler_params=pltpu.CompilerParams(vmem_limit_bytes=16 * 1024 * 1024),
        cost_estimate=pl.CostEstimate(
            flops=1_000_000_000, bytes_accessed=1_000_000, transcendentals=600_000
        ),
        name="outer",
    )(
        inner, outer, spread, norm_gains, taps, embed_table, point_weight, query_weight, key_weight, x, n
    )

    own_keys = lax.all_to_all(keys, ("x_hi", "z"), 0, 0, tiled=False)
    other_keys = lax.ppermute(own_keys, "core", [(0, 1), (1, 0)])

    weights, trunk = pl.pallas_call(
        weights_kernel,
        out_shape=(
            jax.ShapeDtypeStruct((8, 3 * PC, 2 * PC), BF16),
            jax.ShapeDtypeStruct((SLAB, C), BF16),
        ),
        in_specs=vmem(3),
        out_specs=(vmem(1)[0], pl.BlockSpec(memory_space=pl.ANY)),
        scratch_shapes=[pltpu.VMEM((18, PC, PC), BF16), pltpu.SemaphoreType.DMA],
        compiler_params=pltpu.CompilerParams(vmem_limit_bytes=8 * 1024 * 1024),
        cost_estimate=pl.CostEstimate(
            flops=400_000_000, bytes_accessed=2_000_000, transcendentals=0
        ),
        name="weights",
    )(queries, pair_kernel, trunk)
    pair_map = pl.pallas_call(
        pair_kernel_body,
        out_shape=jax.ShapeDtypeStruct((16, 512, PC), BF16),
        in_specs=vmem(4),
        out_specs=pl.BlockSpec(memory_space=pl.ANY),
        scratch_shapes=[
            pltpu.VMEM((512, 3 * PC), BF16),
            pltpu.VMEM((512, PC), F32),
            pltpu.VMEM((16, 512, PC), BF16),
            pltpu.SemaphoreType.DMA((8,)),
        ],
        compiler_params=pltpu.CompilerParams(vmem_limit_bytes=16 * 1024 * 1024),
        name="pair",
    )(queries, own_keys, other_keys, weights)
    return (trunk, pair_map)


def solution(mesh):
    devices = mesh.devices.reshape(2, 8, 2, -1)
    fine = Mesh(devices, ("x_hi", "z", "core", "batch"))
    rows = ("batch", "x_hi", "z", "core")
    return jax.shard_map(
        on_device,
        mesh=fine,
        in_specs=(P(rows, None), P(), P(), P(), P(), P(), P(), P()),
        out_specs=(P(rows, None), P(rows, None, None)),
        check_vma=False,
    )
```

```python
import math

import jax
import jax.numpy as jnp
from jax import lax
from jax.experimental import pallas as pl
from jax.experimental.pallas import tpu as pltpu
from jax.sharding import Mesh
from jax.sharding import PartitionSpec as P

F32 = jnp.float32
BF16 = jnp.bfloat16
C = 768
PC = 128
BASES = 128
BINS = 8192
SLAB = 256
POOL = 16
HALO = 112
ROWS = SLAB + 2 * HALO
DILATIONS = (2, 8, 32)
STEP = 16

GELU_A = math.sqrt(2.0 / math.pi)
GELU_B = 0.044715 * GELU_A


def gelu_of_half(half):
    half = half.astype(BF16)
    squared = half * half
    inner = half * (jnp.asarray(2.0 * GELU_A, BF16) + jnp.asarray(8.0 * GELU_B, BF16) * squared)
    return half + half * jnp.tanh(inner)


def spread_matrix():
    return (
        lax.broadcasted_iota(jnp.int32, (BASES, 4 * BASES), 1) // 4
        == lax.broadcasted_iota(jnp.int32, (BASES, 4 * BASES), 0)
    ).astype(F32).astype(BF16)


def one_hot_rows(codes, spread):
    repeated = jnp.dot(codes, spread, preferred_element_type=F32)
    base = (lax.broadcasted_iota(jnp.int32, repeated.shape, 1) % 4).astype(F32)
    return jnp.where(repeated == base, 1.0, 0.0).astype(BF16)


def rows_at(base, offset, count):
    return pl.ds(base + offset, count)


def norm_rows(x_ref, n_ref, layer, base, count, scales=None):
    for k in range(count // STEP):
        at = rows_at(base, k * STEP, STEP)
        rows = x_ref[at, :]
        mean = jnp.sum(rows * rows, axis=-1, keepdims=True) * (1.0 / C)
        factor = lax.rsqrt(mean + 1e-06)
        if scales is not None and scales[k] is not None:
            factor = factor * scales[k]
        rows = rows * factor
        for c in range(C // 128):
            n_ref[layer, c, at, :] = rows[:, c * 128 : (c + 1) * 128]


def spread_taps(taps, gains, wide_taps):
    for layer in range(3):
        gain = gains[layer : layer + 1, :] * 0.5
        for t in range(5):
            row = taps[t, layer : layer + 1, :] * gain
            wide_taps[layer, t] = jnp.broadcast_to(row, (8, C))


def conv_rows(n_ref, a_ref, layer, wide_taps, base, count, to):
    reach = DILATIONS[layer]
    for k in range(0, count, STEP):
        for c in range(C // 128):
            cols = slice(c * 128, (c + 1) * 128)
            halves = []
            for row in (k, k + 8):
                half = None
                for t in range(5):
                    piece = n_ref[layer, c, rows_at(base, row + (t - 2) * reach, 8), :]
                    term = piece * wide_taps[layer, t, :, cols]
                    half = term if half is None else half + term
                halves.append(half)
            half = jnp.concatenate(halves, axis=0)
            a_ref[to + k : to + k + STEP, cols] = gelu_of_half(half)


def mix(a_ref, x_ref, weights, base, count, to):
    at = rows_at(base, 0, count)
    for strip in range(3):
        cols = slice(strip * 256, strip * 256 + 256)
        update = jnp.dot(a_ref[to : to + count, :], weights[:, cols], preferred_element_type=F32)
        x_ref[at, cols] = x_ref[at, cols] + update


def ends_kernel(bases_hbm, to_core, to_chip, codes, spread, own, sem):
    copy = pltpu.make_async_copy(bases_hbm, own, sem)
    copy.start()
    spread[...] = spread_matrix()
    core = lax.axis_index("core")
    copy.wait()
    rows = own[...].astype(F32)
    head = rows[:HALO].astype(BF16)
    tail = rows[SLAB - HALO :].astype(BF16)
    to_core[...] = jnp.where(core == 0, tail, head)
    to_chip[...] = jnp.where(core == 0, head, tail)
    codes[...] = rows.astype(BF16)


def inner_kernel(codes, spread, table, gains, taps, point, x_ref, n_ref, wide_taps, a_ref):
    one_hot = one_hot_rows(codes[...], spread[...])
    x_ref[HALO : HALO + SLAB, :] = jnp.dot(one_hot, table[...], preferred_element_type=F32)
    spread_taps(taps, gains, wide_taps)
    norm_rows(x_ref, n_ref, 0, 112, 256)
    for layer, low, high in ((0, 128, 352), (1, 144, 336)):
        middle = (low + high) // 2
        for start, stop in ((low, middle), (middle, high)):
            conv_rows(n_ref, a_ref, layer, wide_taps, start, stop - start, start - low)
            mix(a_ref, x_ref, point.at[layer], start, stop - start, start - low)
            norm_rows(x_ref, n_ref, layer + 1, start, stop - start)


def side_base(far, low, high):
    core = lax.axis_index("core")
    return pl.multiple_of(jnp.where((core == 0) == far, low, high), STEP)


def near_kernel(
    codes, spread, wide_taps, table, point, x_in, n_in,
    x_ref, n_ref, a_ref,
):
    del x_in, n_in
    one_hot = one_hot_rows(codes[...], spread[...])
    base = side_base(False, 0, 368)
    x_ref[rows_at(base, 0, HALO), :] = jnp.dot(one_hot, table[...], preferred_element_type=F32)
    norm_rows(x_ref, n_ref, 0, base, HALO)
    base = side_base(False, 16, 352)
    conv_rows(n_ref, a_ref, 0, wide_taps, base, HALO, 0)
    mix(a_ref, x_ref, point.at[0], base, HALO, 0)
    norm_rows(x_ref, n_ref, 1, base, HALO)
    conv_rows(n_ref, a_ref, 2, wide_taps, 208, 64, HALO)
    base = side_base(False, 32, 336)
    conv_rows(n_ref, a_ref, 1, wide_taps, base, HALO, 0)
    mix(a_ref, x_ref, point.at[1], base, HALO, 0)
    norm_rows(x_ref, n_ref, 2, base, HALO)
    base = side_base(False, 96, 272)
    conv_rows(n_ref, a_ref, 2, wide_taps, base, HALO, 0)
    mix(a_ref, x_ref, point.at[2], base, HALO, 0)
    mix(a_ref, x_ref, point.at[2], 208, 64, HALO)


def far_kernel(
    codes, spread, wide_taps, table, point, query_w, key_w, x_in, n_in,
    trunk_out, keys_out, query_out, x_ref, n_ref, a_ref,
):
    del x_in, n_in
    place = lax.axis_index(("x_hi", "z", "core"))
    core = lax.axis_index("core")
    one_hot = one_hot_rows(codes[...], spread[...])
    base = side_base(True, 0, 368)
    x_ref[rows_at(base, 0, HALO), :] = jnp.dot(one_hot, table[...], preferred_element_type=F32)
    beyond = (place == 0) | (place == 31)
    gone = jnp.where(beyond, 0.0, 1.0)
    gone_low = jnp.where(beyond & (core == 0), 0.0, 1.0)
    gone_high = jnp.where(beyond & (core == 1), 0.0, 1.0)

    norm_rows(x_ref, n_ref, 0, base, HALO, [gone] * 7)
    base = side_base(True, 16, 352)
    conv_rows(n_ref, a_ref, 0, wide_taps, base, HALO, 0)
    mix(a_ref, x_ref, point.at[0], base, HALO, 0)
    norm_rows(x_ref, n_ref, 1, base, HALO, [gone_low] + [gone] * 5 + [gone_high])
    base = side_base(True, 32, 336)
    conv_rows(n_ref, a_ref, 1, wide_taps, base, HALO, 0)
    mix(a_ref, x_ref, point.at[1], base, HALO, 0)
    norm_rows(x_ref, n_ref, 2, base, HALO, [gone_low] * 2 + [gone] * 3 + [gone_high] * 2)
    base = side_base(True, 96, 272)
    conv_rows(n_ref, a_ref, 2, wide_taps, base, HALO, 0)
    mix(a_ref, x_ref, point.at[2], base, HALO, 0)

    trunk = x_ref[96:384, :].astype(BF16)
    trunk_out[...] = trunk[POOL : POOL + SLAB, :]
    pooling = jnp.where(
        lax.broadcasted_iota(jnp.int32, (32, 288), 1) // POOL
        == lax.broadcasted_iota(jnp.int32, (32, 288), 0),
        1.0 / POOL,
        0.0,
    ).astype(BF16)
    pooled = jnp.dot(pooling, trunk, preferred_element_type=F32).astype(BF16)
    queries = jnp.dot(pooled, query_w[...], preferred_element_type=F32).astype(BF16).astype(F32)
    keys = jnp.dot(pooled, key_w[...], preferred_element_type=F32)
    row = place * (SLAB // POOL) - 1 + lax.broadcasted_iota(jnp.int32, (32, PC), 0)
    query_out[...] = jnp.where((row >= 0) & (row < BINS // POOL), queries, 0.0)
    mine = pltpu.roll(keys, 31, 0)[0:16].astype(BF16)
    for peer in range(16):
        keys_out[peer] = mine


def weights_kernel(queries, kernel, trunk, weights, trunk_hbm, wide_q, sem):
    copy = pltpu.make_async_copy(trunk, trunk_hbm, sem)
    copy.start()
    flipped = jnp.transpose(queries[...], (1, 0)) * 0.5
    for i in range(18):
        wide_q[i] = jnp.broadcast_to(flipped[:, i : i + 1], (PC, PC)).astype(BF16)

    def two_rows(i, _):
        for r in range(2):
            row = 2 * i + r
            for b in range(3):
                mixed = wide_q[row] * kernel[0, b]
                mixed = mixed + wide_q[row + 1] * kernel[1, b]
                mixed = mixed + wide_q[row + 2] * kernel[2, b]
                weights[i, b * PC : (b + 1) * PC, r * PC : (r + 1) * PC] = mixed
        return 0

    lax.fori_loop(0, 8, two_rows, 0)
    copy.wait()


def pair_kernel_body(queries, own, other, weights, out_hbm, key_cat, key_f, out_ref, sems):
    core = lax.axis_index("core")
    for g in range(16):
        mine = own[g]
        theirs = other[g]
        key_cat[g * 32 : g * 32 + 16, PC : 2 * PC] = jnp.where(core == 0, mine, theirs)
        key_cat[g * 32 + 16 : g * 32 + 32, PC : 2 * PC] = jnp.where(core == 0, theirs, mine)
    keys = key_cat[:, PC : 2 * PC].astype(F32)
    key_f[...] = keys
    at = lax.broadcasted_iota(jnp.int32, keys.shape, 0)
    before = jnp.where(at == 0, 0.0, pltpu.roll(keys, 1, 0))
    after = jnp.where(at == 511, 0.0, pltpu.roll(keys, 511, 0))
    key_cat[:, 0:PC] = before.astype(BF16)
    key_cat[:, 2 * PC : 3 * PC] = after.astype(BF16)

    def copy_of(i):
        return pltpu.make_async_copy(
            out_ref.at[pl.ds(2 * i, 2)], out_hbm.at[pl.ds(2 * i, 2)], sems.at[i]
        )

    for i in range(8):
        query_rows = [queries[2 * i + r + 1 : 2 * i + r + 2, :].astype(BF16) for r in range(2)]
        for m in range(2):
            rows = slice(m * 256, m * 256 + 256)
            half = jnp.dot(key_cat[rows, :], weights[i], preferred_element_type=F32)
            key = key_f[rows, :].astype(BF16)
            for r in range(2):
                gelu = gelu_of_half(half[:, r * PC : (r + 1) * PC])
                out_ref[2 * i + r, rows, :] = key * query_rows[r] + gelu
        copy_of(i).start()

    def finish(i, _):
        copy_of(i).wait()
        return 0

    lax.fori_loop(0, 8, finish, 0)


def in_hbm(array):
    return pltpu.with_memory_space_constraint(array, pltpu.HBM)


def vmem(count):
    return [pl.BlockSpec(memory_space=pltpu.VMEM)] * count


def on_device(
    bases, embed_table, norm_gains, depth_taps, point_weight, query_weight, key_weight, pair_kernel
):
    seq = ("x_hi", "z", "core")
    outer_pairs = []
    for i in range(1, 31, 2):
        outer_pairs += [(i, i + 1), (i + 1, i)]
    to_core, to_chip, codes, spread = pl.pallas_call(
        ends_kernel,
        out_shape=(
            jax.ShapeDtypeStruct((HALO, BASES), BF16),
            jax.ShapeDtypeStruct((HALO, BASES), BF16),
            jax.ShapeDtypeStruct((SLAB, BASES), BF16),
            jax.ShapeDtypeStruct((BASES, 4 * BASES), BF16),
        ),
        in_specs=[pl.BlockSpec(memory_space=pltpu.HBM)],
        out_specs=tuple(vmem(4)),
        scratch_shapes=[pltpu.VMEM((SLAB, BASES), jnp.int32), pltpu.SemaphoreType.DMA],
        compiler_params=pltpu.CompilerParams(vmem_limit_bytes=4 * 1024 * 1024),
        cost_estimate=pl.CostEstimate(
            flops=20_000_000_000, bytes_accessed=1_000_000, transcendentals=0
        ),
        name="ends",
    )(in_hbm(bases))
    inner = lax.ppermute(to_core, "core", [(0, 1), (1, 0)])
    outer = lax.ppermute(to_chip, seq, outer_pairs)

    taps = jnp.transpose(depth_taps, (1, 0, 2))
    state = (
        jax.ShapeDtypeStruct((ROWS, C), F32),
        jax.ShapeDtypeStruct((3, C // 128, ROWS, 128), F32),
    )
    x, n, wide_taps = pl.pallas_call(
        inner_kernel,
        out_shape=state + (jax.ShapeDtypeStruct((3, 5, 8, C), F32),),
        in_specs=vmem(6),
        out_specs=tuple(vmem(3)),
        scratch_shapes=[pltpu.VMEM((SLAB, C), BF16)],
        compiler_params=pltpu.CompilerParams(vmem_limit_bytes=12 * 1024 * 1024),
        cost_estimate=pl.CostEstimate(
            flops=800_000_000, bytes_accessed=5_000_000, transcendentals=400_000
        ),
        name="inner",
    )(codes, spread, embed_table, norm_gains, taps, point_weight)
    x, n = pl.pallas_call(
        near_kernel,
        out_shape=state,
        in_specs=vmem(7),
        out_specs=tuple(vmem(2)),
        scratch_shapes=[pltpu.VMEM((288, C), BF16)],
        input_output_aliases={5: 0, 6: 1},
        compiler_params=pltpu.CompilerParams(vmem_limit_bytes=12 * 1024 * 1024),
        cost_estimate=pl.CostEstimate(
            flops=600_000_000, bytes_accessed=1_000_000, transcendentals=300_000
        ),
        name="near",
    )(inner, spread, wide_taps, embed_table, point_weight, x, n)
    trunk, keys, queries, _, _ = pl.pallas_call(
        far_kernel,
        out_shape=(
            jax.ShapeDtypeStruct((SLAB, C), BF16),
            jax.ShapeDtypeStruct((16, 16, PC), BF16),
            jax.ShapeDtypeStruct((32, PC), F32),
        )
        + state,
        in_specs=vmem(9),
        out_specs=tuple(vmem(5)),
        scratch_shapes=[pltpu.VMEM((288, C), BF16)],
        input_output_aliases={7: 3, 8: 4},
        compiler_params=pltpu.CompilerParams(vmem_limit_bytes=12 * 1024 * 1024),
        cost_estimate=pl.CostEstimate(
            flops=600_000_000, bytes_accessed=1_000_000, transcendentals=300_000
        ),
        name="far",
    )(
        outer, spread, wide_taps, embed_table, point_weight, query_weight, key_weight, x, n
    )

    own_keys = lax.all_to_all(keys, ("x_hi", "z"), 0, 0, tiled=False)
    other_keys = lax.ppermute(own_keys, "core", [(0, 1), (1, 0)])

    weights, trunk = pl.pallas_call(
        weights_kernel,
        out_shape=(
            jax.ShapeDtypeStruct((8, 3 * PC, 2 * PC), BF16),
            jax.ShapeDtypeStruct((SLAB, C), BF16),
        ),
        in_specs=vmem(3),
        out_specs=(vmem(1)[0], pl.BlockSpec(memory_space=pl.ANY)),
        scratch_shapes=[pltpu.VMEM((18, PC, PC), BF16), pltpu.SemaphoreType.DMA],
        compiler_params=pltpu.CompilerParams(vmem_limit_bytes=8 * 1024 * 1024),
        cost_estimate=pl.CostEstimate(
            flops=400_000_000, bytes_accessed=2_000_000, transcendentals=0
        ),
        name="weights",
    )(queries, pair_kernel, trunk)
    pair_map = pl.pallas_call(
        pair_kernel_body,
        out_shape=jax.ShapeDtypeStruct((16, 512, PC), BF16),
        in_specs=vmem(4),
        out_specs=pl.BlockSpec(memory_space=pl.ANY),
        scratch_shapes=[
            pltpu.VMEM((512, 3 * PC), BF16),
            pltpu.VMEM((512, PC), F32),
            pltpu.VMEM((16, 512, PC), BF16),
            pltpu.SemaphoreType.DMA((8,)),
        ],
        compiler_params=pltpu.CompilerParams(vmem_limit_bytes=16 * 1024 * 1024),
        name="pair",
    )(queries, own_keys, other_keys, weights)
    return (trunk, pair_map)


def solution(mesh):
    devices = mesh.devices.reshape(2, 8, 2, -1)
    fine = Mesh(devices, ("x_hi", "z", "core", "batch"))
    rows = ("batch", "x_hi", "z", "core")
    return jax.shard_map(
        on_device,
        mesh=fine,
        in_specs=(P(rows, None), P(), P(), P(), P(), P(), P(), P()),
        out_specs=(P(rows, None), P(rows, None, None)),
        check_vma=False,
    )
```
